32 devices in a mesh: wide: 8 (over z, y), narrow: 4 (over x, core).
Axes of the slice: x: 2, y: 2, z: 4, core: 2. Of those that a mesh axis runs over, the one named last changes fastest.
Arguments:
- tokens: bfloat16 [32, 256, 1024], P(('wide', 'narrow')), may hold values from -6 to 6
- segment_ids: int32 [32, 256], P(('wide', 'narrow')), may hold values from 0 to 3, never falling along the last dimension, each value on 1 to 128 neighbouring positions
- routed_index: int32 [32, 32], P(('wide', 'narrow')), may hold values from 0 to 255, as said below
- out_grad: bfloat16 [32, 256, 1024], P(('wide', 'narrow')), may hold values from -6 to 6
- dense_attn_gain: bfloat16 [1024], P('wide'), may hold values from 0.5 to 1.5
- dense_qkv: bfloat16 [1024, 3072], P('wide'), may hold values from -0.1875 to 0.1875
- dense_proj: bfloat16 [1024, 1024], P('wide'), may hold values from -0.75 to 0.75
- dense_mlp_gain: bfloat16 [1024], P('wide'), may hold values from 0.5 to 1.5
- dense_up: bfloat16 [1024, 4096], P('wide'), may hold values from -0.1875 to 0.1875
- dense_down: bfloat16 [4096, 1024], P('wide'), may hold values from -0.09375 to 0.09375
- routed_attn_gain: bfloat16 [1024], P('wide'), may hold values from 0.5 to 1.5
- routed_qkv: bfloat16 [1024, 3072], P('wide'), may hold values from -0.1875 to 0.1875
- routed_proj: bfloat16 [1024, 1024], P('wide'), may hold values from -0.75 to 0.75
- routed_mlp_gain: bfloat16 [1024], P('wide'), may hold values from 0.5 to 1.5
- routed_up: bfloat16 [1024, 4096], P('wide'), may hold values from -0.1875 to 0.1875
- routed_down: bfloat16 [4096, 1024], P('wide'), may hold values from -0.09375 to 0.09375
- router_vector: bfloat16 [1024], replicated, may hold values from -0.1875 to 0.1875
Outputs:
- result: bfloat16 [32, 256, 1024], P(('wide', 'narrow'))
- input_grad: bfloat16 [32, 256, 1024], P(('wide', 'narrow'))
- grad_dense_attn_gain: float32 [1024], P('wide')
- grad_dense_qkv: float32 [1024, 3072], P('wide')
- grad_dense_proj: float32 [1024, 1024], P('wide')
- grad_dense_mlp_gain: float32 [1024], P('wide')
- grad_dense_up: float32 [1024, 4096], P('wide')
- grad_dense_down: float32 [4096, 1024], P('wide')
- grad_routed_attn_gain: float32 [1024], P('wide')
- grad_routed_qkv: float32 [1024, 3072], P('wide')
- grad_routed_proj: float32 [1024, 1024], P('wide')
- grad_routed_mlp_gain: float32 [1024], P('wide')
- grad_routed_up: float32 [1024, 4096], P('wide')
- grad_routed_down: float32 [4096, 1024], P('wide')
- router_grad: float32 [1024], replicated
The draws below stay inside these ranges and needn't reach their ends.
Inputs may be any that keep to these rules, and one draw needn't show every extreme that they name: `routed_index`: each row holds 32 distinct positions of its sequence in increasing order.
All inputs are finite; a program needn't handle non-finite values.
Results may differ from the reference program's by a relative error of at most 0.022.
Values may be sent and summed in bfloat16 or wider, within the bound.
No kernel may reach another device: no remote copies, remote signals or barrier semaphores. Data moves between devices by JAX's collectives and lax.ppermute only.
A program may use at most 256 MiB of HBM per device.

```python
import math
import jax
import jax.numpy as jnp
import numpy as np
from jax import lax

D = 1024
HEADS = 16
HDIM = 64
FF = 4096
SEQ = 256
CAP = 32
SEQS = 32


def draw_routed_index(key, part):
    keys_all = jax.random.split(key, SEQS)

    def pick_rows(row_key):
        return jnp.sort(jax.random.permutation(row_key, SEQ)[:CAP]).astype(jnp.int32)
    return jax.vmap(pick_rows)(keys_all)


def level_of(own_key, extent, cuts, low, top_value):
    level, own = 1.0, jax.random.fold_in(own_key, 6)
    for axis_at, blocks in cuts:
        heights = jnp.exp(jax.random.uniform(jax.random.fold_in(own, axis_at), (blocks,), jnp.float32, low / len(cuts), top_value / len(cuts)))
        level = level * jnp.repeat(heights, extent[axis_at] // blocks).reshape([-1 if axis == axis_at else 1 for axis in range(len(extent))])
    return level


def profile(number_of, total, most, lean):
    weights = [(1 << 20) // math.isqrt(grade ** lean) + 1 for grade in range(2, number_of + 1)]
    surplus, given = total - most - (number_of - 1), [1] * (number_of - 1)
    while surplus > 0:
        free = [i for i in range(number_of - 1) if given[i] < most]
        mass, remaining = sum([weights[i] for i in free]), surplus
        for i in free:
            extra = min(most - given[i], max(1, remaining * weights[i] // mass), surplus)
            given[i] = given[i] + extra
            surplus = surplus - extra
    return np.array([most] + given)


def uneven_parts(own_key, number_of, total, limit, slope):
    if number_of == 2:
        one = jax.random.randint(own_key, (), max(1, total - limit), min(limit, total - 1) + 1)
        return jnp.stack([one, total - one])
    lengths = jnp.asarray(profile(number_of, total, limit, slope), jnp.int32)
    pairs = (number_of - 1) // 2
    source_of, sink = lengths[1:1 + 2 * pairs:2], lengths[2:2 + 2 * pairs:2]
    slack = jnp.minimum(source_of - 1, limit - sink)
    passed = jax.random.randint(jax.random.fold_in(own_key, 1), (pairs,), 0, 1 << 20) % (slack + 1)
    lengths = lengths.at[1:1 + 2 * pairs:2].set(source_of - passed).at[2:2 + 2 * pairs:2].set(sink + passed)
    return lengths[jax.random.permutation(jax.random.fold_in(own_key, 2), number_of)]


def gaussian(own_key, extent, width, limit, cuts=(), kind=jnp.bfloat16):
    drawn = jax.random.normal(own_key, extent, jnp.float32) * width
    if len(cuts) > 0:
        drawn = level_of(own_key, extent, cuts, -0.22, 0.18) * drawn
    return jnp.clip(drawn, min=-limit, max=limit).astype(kind)


def setup_inputs(seed: int = 0) -> dict:
    keys = jax.random.split(jax.random.key(seed), 18)
    return {
        "tokens": gaussian(keys[0], (SEQS, SEQ, D), 1.0, 6.0, ((0, 32),)),
        "segment_ids": jax.vmap(lambda own: jnp.searchsorted(jnp.cumsum(uneven_parts(own, 4, SEQ, SEQ // 2, 1)), jnp.arange(SEQ), side="right"))(jax.random.split(keys[1], SEQS)).reshape((SEQS, SEQ)).astype(jnp.int32),
        "routed_index": draw_routed_index(jax.random.fold_in(keys[17], 71), 0),
        "out_grad": gaussian(keys[3], (SEQS, SEQ, D), 1.0, 6.0, ((0, 32),)),
        "dense_attn_gain": jnp.clip(1.0 + 0.1 * jax.random.normal(keys[4], (D,), jnp.float32), 0.5, 1.5).astype(jnp.bfloat16),
        "dense_qkv": gaussian(keys[5], (D, 3 * D), D ** -0.5, 0.1875, ((0, 8),)),
        "dense_proj": gaussian(keys[6], (D, D), (D // 16) ** -0.5, 0.75, ((0, 8),)),
        "dense_mlp_gain": jnp.clip(1.0 + 0.1 * jax.random.normal(keys[7], (D,), jnp.float32), 0.5, 1.5).astype(jnp.bfloat16),
        "dense_up": gaussian(keys[8], (D, FF), D ** -0.5, 0.1875, ((0, 8),)),
        "dense_down": gaussian(keys[9], (FF, D), FF ** -0.5, 0.09375, ((0, 8),)),
        "routed_attn_gain": jnp.clip(1.0 + 0.1 * jax.random.normal(keys[10], (D,), jnp.float32), 0.5, 1.5).astype(jnp.bfloat16),
        "routed_qkv": gaussian(keys[11], (D, 3 * D), D ** -0.5, 0.1875, ((0, 8),)),
        "routed_proj": gaussian(keys[12], (D, D), (D // 16) ** -0.5, 0.75, ((0, 8),)),
        "routed_mlp_gain": jnp.clip(1.0 + 0.1 * jax.random.normal(keys[13], (D,), jnp.float32), 0.5, 1.5).astype(jnp.bfloat16),
        "routed_up": gaussian(keys[14], (D, FF), D ** -0.5, 0.1875, ((0, 8),)),
        "routed_down": gaussian(keys[15], (FF, D), FF ** -0.5, 0.09375, ((0, 8),)),
        "router_vector": gaussian(keys[16], (D,), D ** -0.5, 0.1875),
    }


EPS = 1e-06
NEG = -1e+30
HIGH = lax.Precision.HIGHEST

@jax.custom_vjp
def low(v):
    return lax.optimization_barrier(v.astype(jnp.bfloat16)).astype(jnp.float32)

@jax.custom_vjp
def low_back(v):
    return v

def low_keep(v):
    return (low(v), None)

def low_pass(kept, grad):
    return (grad,)

def back_keep(v):
    return (v, None)

def back_low(kept, grad):
    return (low(grad),)
low.defvjp(low_keep, low_pass)
low_back.defvjp(back_keep, back_low)

def rms_norm(values, gain):
    return values * lax.rsqrt(lax.optimization_barrier(jnp.mean(values * values, -1, keepdims=True)) + EPS) * gain

def matmul(left, right):
    return jnp.dot(left, right, precision=HIGH, preferred_element_type=jnp.float32)

def attend(inputs, gain, mixing, project, positions, segments):
    row_count = inputs.shape[0]
    normed = low(rms_norm(inputs, gain))
    combined = low_back(low(matmul(normed, mixing)))
    parts = combined.reshape(row_count, 3, HEADS, HDIM)
    scores = jnp.einsum('qhd,khd->hqk', parts[:, 0], parts[:, 1], precision=HIGH) * HDIM ** (-0.5)
    scores = low_back(scores)
    allowed = (positions[None, :] <= positions[:, None]) & (segments[None, :] == segments[:, None])
    scores = jnp.where(allowed[None], scores, NEG)
    attn_prob = low(jax.nn.softmax(scores, axis=-1))
    attended = jnp.einsum('hqk,khd->qhd', attn_prob, parts[:, 2], precision=HIGH).reshape(row_count, D)
    attended = low_back(low(attended))
    return low_back(matmul(attended, project))

def feed(inputs, gain, upward, downward):
    normed = low(rms_norm(inputs, gain))
    hidden_pre = low_back(matmul(normed, upward))
    active = low(jax.nn.gelu(hidden_pre, approximate=True))
    return low_back(matmul(active, downward))

def one_sequence(weights, inputs, segments, chosen):
    positions = jnp.arange(SEQ, dtype=jnp.int32)
    hidden = inputs + attend(inputs, weights[0], weights[1], weights[2], positions, segments)
    middle = hidden + feed(hidden, weights[3], weights[4], weights[5])
    selected = middle[chosen]
    chosen_seg = segments[chosen]
    rate = jax.nn.sigmoid(jnp.dot(selected, weights[12], precision=HIGH))
    routed_att = attend(selected, weights[6], weights[7], weights[8], chosen, chosen_seg)
    change = routed_att + feed(selected + routed_att, weights[9], weights[10], weights[11])
    return middle.at[chosen].add(rate[:, None] * change)

def reference(tokens, segment_ids, routed_index, out_grad, dense_attn_gain, dense_qkv, dense_proj, dense_mlp_gain, dense_up, dense_down, routed_attn_gain, routed_qkv, routed_proj, routed_mlp_gain, routed_up, routed_down, router_vector):
    weights = tuple((matrix.astype(jnp.float32) for matrix in (dense_attn_gain, dense_qkv, dense_proj, dense_mlp_gain, dense_up, dense_down, routed_attn_gain, routed_qkv, routed_proj, routed_mlp_gain, routed_up, routed_down, router_vector)))

    def forward(params, inputs):

        def apply(packed):
            return jax.checkpoint(one_sequence)(params, packed[0], packed[1], packed[2])
        return lax.map(apply, (inputs, segment_ids, routed_index))
    result, pull = jax.vjp(forward, weights, tokens.astype(jnp.float32))
    weight_grads, input_grad = pull(out_grad.astype(jnp.float32))
    return (result.astype(jnp.bfloat16), input_grad.astype(jnp.bfloat16), weight_grads[0], weight_grads[1], weight_grads[2], weight_grads[3], weight_grads[4], weight_grads[5], weight_grads[6], weight_grads[7], weight_grads[8], weight_grads[9], weight_grads[10], weight_grads[11], weight_grads[12])
```

```python
import jax
import jax.numpy as jnp
from jax import lax
from jax.sharding import PartitionSpec as P

HEADS = 16
EPS = 1e-06
NEG = -1e30
HIGH = lax.Precision.HIGHEST
LOW = jnp.bfloat16
F32 = jnp.float32


def dot_rows(left, right):
    return jnp.dot(left, right, preferred_element_type=F32)


def dot_cross(left, right):
    return lax.dot_general(left, right, (((0,), (0,)), ((), ())), preferred_element_type=F32)


def dot_back(left, right):
    return lax.dot_general(left, right, (((1,), (1,)), ((), ())), preferred_element_type=F32)


def bits_of(size):
    found = []
    bit = size // 2
    while bit >= 1:
        found.append(bit)
        bit //= 2
    return found


def xor_blocks(array, index, blocks, axis):
    size = array.shape[axis] // blocks
    for bit in bits_of(blocks):
        parts = [
            lax.slice_in_dim(array, k * size, (k + 1) * size, axis=axis) for k in range(blocks)
        ]
        swapped = jnp.concatenate([parts[k ^ bit] for k in range(blocks)], axis=axis)
        array = jnp.where((index & bit) != 0, swapped, array)
    return array


class Links:
    def __init__(self, sizes, depth):
        self.sizes = sizes
        self.depth = depth
        self.sent = {}

    def swap(self, array, axis, bit):
        queue = self.sent.setdefault((axis, bit), [])
        if self.depth and len(queue) >= self.depth:
            array, queue[-self.depth] = lax.optimization_barrier((array, queue[-self.depth]))
        size = self.sizes[axis]
        got = lax.ppermute(array, axis, [(i, i ^ bit) for i in range(size)])
        queue.append(got)
        return got

    def gather(self, piece, axis, order):
        have = {0: piece}
        for bit in order:
            have.update({k ^ bit: self.swap(v, axis, bit) for k, v in list(have.items())})
        return have

    def scatter(self, pieces, axis, order):
        have = dict(pieces)
        for bit in order:
            kept = {}
            for k in [k for k in have if not k & bit]:
                other = self.swap(have[k ^ bit].astype(LOW), axis, bit)
                kept[k] = have[k].astype(F32) + other.astype(F32)
            have = kept
        return have[0]


def in_order(have, axis=0):
    return jnp.concatenate([have[k] for k in sorted(have)], axis=axis)


def split_rows(array, count):
    size = array.shape[0] // count
    return {k: array[k * size : (k + 1) * size] for k in range(count)}


def norm_stats(values):
    return lax.rsqrt(jnp.mean(values * values, -1, keepdims=True) + EPS)


def norm_back(values, scale, gain, grad):
    weighted = grad * gain
    inner = jnp.mean(weighted * values, -1, keepdims=True)
    return scale * (weighted - values * (scale * scale) * inner)


def gelu_parts(v):
    root = 0.7978845608028654
    inner = jnp.tanh(root * (v + 0.044715 * v * v * v))
    value = 0.5 * v * (1.0 + inner)
    slope = 0.5 * (1.0 + inner) + 0.5 * v * (1.0 - inner * inner) * root * (
        1.0 + 3.0 * 0.044715 * v * v
    )
    return value, slope


def attend_prob(queries, keys, allowed):
    scores = jnp.einsum("sqhd,skhd->shqk", queries, keys, preferred_element_type=F32)
    scores = jnp.where(allowed, scores * queries.shape[-1] ** (-0.5), NEG)
    lifted = jnp.exp(scores - jnp.max(scores, -1, keepdims=True))
    return lifted / jnp.sum(lifted, -1, keepdims=True)


def heads_of(combined, seqs, heads):
    rows, width = combined.shape
    parts = combined.reshape(seqs, rows // seqs, 3, heads, width // (3 * heads))
    return parts[:, :, 0], parts[:, :, 1], parts[:, :, 2]


def attend_forward(combined, allowed, seqs, heads):
    queries, keys, vals = heads_of(combined, seqs, heads)
    prob = attend_prob(queries, keys, allowed).astype(LOW)
    out = jnp.einsum("shqk,skhd->sqhd", prob, vals, preferred_element_type=F32)
    return out.reshape(combined.shape[0], -1).astype(LOW)


def attend_backward(combined, allowed, seqs, heads, out_grad):
    queries, keys, vals = heads_of(combined, seqs, heads)
    grad = out_grad.reshape(queries.shape)
    scale = queries.shape[-1] ** (-0.5)
    prob = attend_prob(queries, keys, allowed)
    prob_grad = jnp.einsum("sqhd,skhd->shqk", grad, vals, preferred_element_type=F32)
    inner = jnp.sum(prob * prob_grad, -1, keepdims=True)
    score_grad = (prob * (prob_grad - inner)).astype(LOW)
    query_grad = jnp.einsum("shqk,skhd->sqhd", score_grad, keys, preferred_element_type=F32)
    key_grad = jnp.einsum("shqk,sqhd->skhd", score_grad, queries, preferred_element_type=F32)
    val_grad = jnp.einsum(
        "shqk,sqhd->skhd", prob.astype(LOW), grad, preferred_element_type=F32
    )
    stacked = jnp.stack([query_grad * scale, key_grad * scale, val_grad], 2)
    return stacked.reshape(combined.shape).astype(LOW)


def make_device(wide, narrow):
    wide_bits = bits_of(wide)
    narrow_bits = bits_of(narrow)
    last = wide_bits[-1]
    side = wide_bits[-2] if len(wide_bits) > 1 else last
    order_a = list(wide_bits)
    order_b = wide_bits[:-2] + [last, side] if len(wide_bits) > 1 else order_a

    def per_device(
        tokens,
        segment_ids,
        routed_index,
        out_grad,
        dense_attn_gain,
        dense_qkv,
        dense_proj,
        dense_mlp_gain,
        dense_up,
        dense_down,
        routed_attn_gain,
        routed_qkv,
        routed_proj,
        routed_mlp_gain,
        routed_up,
        routed_down,
        router_vector,
    ):
        sizes = {"wide": wide, "narrow": narrow}
        weights_in = Links(sizes, 2)
        grads_out = Links(sizes, 2)
        acts = Links(sizes, 0)
        w = lax.axis_index("wide")
        n = lax.axis_index("narrow")
        inputs = tokens[0].astype(F32)
        rows, width = inputs.shape
        segments = segment_ids[0]
        chosen = routed_index[0]
        cap = chosen.shape[0]
        heads = HEADS // narrow
        own = width // wide
        ffn = dense_up.shape[1]

        def pick(array, axis):
            return lax.dynamic_index_in_dim(array, n, axis, keepdims=False)

        def quarter_qkv(weight):
            return pick(weight.reshape(own, 3, narrow, width // narrow), 2).reshape(own, -1)

        def quarter_proj(weight):
            return pick(weight.reshape(own, narrow, width // narrow), 1)

        def quarter_up(weight):
            return pick(weight.reshape(own, wide, narrow, ffn // (wide * narrow)), 2).reshape(
                own, -1
            )

        def quarter_down(weight):
            return pick(weight.reshape(narrow, -1, width), 0)

        gains = jnp.stack([dense_attn_gain, dense_mlp_gain, routed_attn_gain, routed_mlp_gain])
        have = acts.gather(gains, "wide", order_a)
        gain_full = xor_blocks(in_order(have, axis=1), w, wide, 1).astype(F32)

        def fetch_proj(weight):
            cols = in_order(weights_in.gather(quarter_proj(weight), "wide", order_a))
            cols = xor_blocks(cols, w, wide, 0).reshape(narrow, width // narrow, -1)
            got = {}
            for k in range(narrow):
                block = lax.dynamic_index_in_dim(cols, n ^ k, 0, keepdims=False)
                got[k] = block if k == 0 else acts.swap(block, "narrow", k)
            return xor_blocks(in_order(got, axis=1), n, narrow, 1)

        def fetch_block(qkv, proj, up, down):
            qkv_full = in_order(weights_in.gather(quarter_qkv(qkv), "wide", order_b))
            proj_full = fetch_proj(proj)
            up_full = in_order(weights_in.gather(quarter_up(up), "wide", order_a))
            down_full = in_order(weights_in.gather(quarter_down(down), "wide", order_a))
            return qkv_full, proj_full, up_full, xor_blocks(down_full, w, wide, 0)

        def share(local):
            return in_order(acts.gather(local, "narrow", narrow_bits))

        def total(partial):
            pieces = split_rows(partial, narrow)
            return acts.scatter(pieces, "narrow", narrow_bits[::-1])

        def normed_share(values, scale, gain):
            normed = (values * scale * gain).astype(LOW)
            return share(xor_blocks(normed, w, wide, 1))

        def attend_layer(values, gain, qkv, proj, allowed):
            scale = norm_stats(values)
            normed = normed_share(values, scale, gain)
            combined = dot_rows(normed, qkv).astype(LOW)
            attended = attend_forward(combined, allowed, narrow, heads)
            branch = total(dot_rows(attended, proj))
            return branch, (values, scale, gain, normed, combined, attended)

        def attend_layer_back(grad_all, kept, qkv, proj, allowed):
            values, scale, gain, normed, combined, attended = kept
            attended_grad = dot_back(grad_all, proj).astype(LOW)
            combined_grad = attend_backward(combined, allowed, narrow, heads, attended_grad)
            normed_grad = total(dot_back(combined_grad, qkv))
            proj_grad = dot_cross(attended, grad_all)
            qkv_grad = dot_cross(normed, combined_grad)
            grad = xor_blocks(normed_grad, w, wide, 1)
            return norm_back(values, scale, gain, grad), qkv_grad, proj_grad

        def feed_layer(values, gain, up, down):
            scale = norm_stats(values)
            normed = normed_share(values, scale, gain)
            hidden_pre = dot_rows(normed, up)
            active = gelu_parts(hidden_pre)[0].astype(LOW)
            branch = total(dot_rows(active, down))
            return branch, (values, scale, gain, normed, hidden_pre, active)

        def feed_layer_back(grad_all, kept, up, down):
            values, scale, gain, normed, hidden_pre, active = kept
            active_grad = dot_back(grad_all, down)
            pre_grad = (gelu_parts(hidden_pre)[1] * active_grad).astype(LOW)
            normed_grad = total(dot_back(pre_grad, up))
            down_grad = dot_cross(active, grad_all)
            up_grad = dot_cross(normed, pre_grad)
            grad = xor_blocks(normed_grad, w, wide, 1)
            return norm_back(values, scale, gain, grad), up_grad, down_grad

        def spread(shard):
            have = grads_out.gather(shard.astype(LOW), "narrow", narrow_bits)
            stacked = jnp.stack([have[k] for k in range(narrow)])
            return xor_blocks(stacked, n, narrow, 0).astype(F32)

        def send_rows(grad, order):
            pieces = split_rows(grad.astype(LOW), wide)
            return grads_out.scatter(pieces, "wide", order[::-1])

        def finish_qkv(grad):
            parts = spread(send_rows(grad, order_b)).reshape(narrow, own, 3, width // narrow)
            return parts.transpose(1, 2, 0, 3).reshape(own, 3 * width)

        def finish_up(grad):
            parts = spread(send_rows(grad, order_a)).reshape(narrow, own, wide, -1)
            return parts.transpose(1, 2, 0, 3).reshape(own, ffn)

        def finish_down(grad):
            parts = spread(send_rows(xor_blocks(grad.astype(LOW), w, wide, 0), order_a))
            return parts.reshape(-1, width)

        def finish_proj(grad):
            cols = grad.astype(LOW).reshape(width // narrow, narrow, width // narrow)
            got = {}
            for k in range(narrow):
                block = lax.dynamic_index_in_dim(cols, n ^ k, 1, keepdims=False)
                got[k] = block if k == 0 else acts.swap(block, "narrow", k)
            full = xor_blocks(in_order(got), n, narrow, 0)
            parts = spread(send_rows(xor_blocks(full, w, wide, 0), order_a))
            return parts.transpose(1, 0, 2).reshape(own, width)

        def gain_grad(weight, grad, gain):
            return jnp.sum(weight.astype(F32) * grad, -1) / gain.astype(F32)

        dense_w = fetch_block(dense_qkv, dense_proj, dense_up, dense_down)
        routed_w = fetch_block(routed_qkv, routed_proj, routed_up, routed_down)

        marks = jnp.concatenate([segments, chosen, jnp.take(segments, chosen)])[None]
        marks = share(marks)
        seg_all = marks[:, :rows]
        pos_r = marks[:, rows : rows + cap]
        seg_r = marks[:, rows + cap :]
        pos = jnp.arange(rows, dtype=jnp.int32)
        allowed_d = (pos[None, None, :] <= pos[None, :, None]) & (
            seg_all[:, None, :] == seg_all[:, :, None]
        )
        allowed_r = (pos_r[:, None, :] <= pos_r[:, :, None]) & (
            seg_r[:, None, :] == seg_r[:, :, None]
        )
        allowed_d, allowed_r = allowed_d[:, None], allowed_r[:, None]

        dense_att, kept_att = attend_layer(inputs, gain_full[0], dense_w[0], dense_w[1], allowed_d)
        hidden = inputs + dense_att
        dense_ffn, kept_ffn = feed_layer(hidden, gain_full[1], dense_w[2], dense_w[3])
        middle = hidden + dense_ffn

        selected = jnp.take(middle, chosen, axis=0)
        route_vec = router_vector.astype(F32)
        rate = jax.nn.sigmoid(jnp.dot(selected, route_vec, precision=HIGH))
        routed_att, kept_att_r = attend_layer(
            selected, gain_full[2], routed_w[0], routed_w[1], allowed_r
        )
        routed_ffn, kept_ffn_r = feed_layer(
            selected + routed_att, gain_full[3], routed_w[2], routed_w[3]
        )
        change = routed_att + routed_ffn
        result = middle.at[chosen].add(rate[:, None] * change)

        result_grad = out_grad[0]
        grad_share = share(result_grad)
        picked_grad = jnp.take(result_grad, chosen, axis=0).astype(F32)
        rate_grad = jnp.sum(picked_grad * change, -1)
        change_grad = rate[:, None] * picked_grad
        logit_grad = rate_grad * rate * (1.0 - rate)
        after_grad, up_grad_r, down_grad_r = feed_layer_back(
            share(change_grad.astype(LOW)), kept_ffn_r, routed_w[2], routed_w[3]
        )
        after_grad_total = change_grad + after_grad
        att_in_grad, qkv_grad_r, proj_grad_r = attend_layer_back(
            share(after_grad_total.astype(LOW)), kept_att_r, routed_w[0], routed_w[1], allowed_r
        )
        selected_grad = after_grad + att_in_grad + logit_grad[:, None] * route_vec[None, :]
        router_total = jnp.dot(logit_grad, selected, precision=HIGH)
        for axis, found in (("narrow", narrow_bits), ("wide", wide_bits)):
            for bit in found:
                router_total = router_total + acts.swap(router_total, axis, bit)

        routed_grads = {}
        routed_grads["down"] = finish_down(down_grad_r)
        routed_grads["up"] = finish_up(up_grad_r)
        routed_grads["proj"] = finish_proj(proj_grad_r)
        routed_grads["qkv"] = finish_qkv(qkv_grad_r)

        new_rows = picked_grad + selected_grad
        middle_grad = result_grad.astype(F32).at[chosen].set(new_rows)
        rows_all = share(new_rows.astype(LOW)).reshape(narrow, cap, width)
        seqs = jnp.arange(narrow, dtype=jnp.int32)[:, None]
        middle_low = (
            grad_share.reshape(narrow, rows, width).at[seqs, pos_r].set(rows_all)
        ).reshape(narrow * rows, width)
        hidden_part, up_grad, down_grad = feed_layer_back(
            middle_low, kept_ffn, dense_w[2], dense_w[3]
        )
        dense_grads = {}
        dense_grads["down"] = finish_down(down_grad)
        dense_grads["up"] = finish_up(up_grad)
        hidden_grad = middle_grad + hidden_part
        input_part, qkv_grad, proj_grad = attend_layer_back(
            share(hidden_grad.astype(LOW)), kept_att, dense_w[0], dense_w[1], allowed_d
        )
        dense_grads["proj"] = finish_proj(proj_grad)
        dense_grads["qkv"] = finish_qkv(qkv_grad)
        input_total = hidden_grad + input_part
        return (
            result.astype(LOW)[None],
            input_total.astype(LOW)[None],
            gain_grad(dense_qkv, dense_grads["qkv"], dense_attn_gain),
            dense_grads["qkv"],
            dense_grads["proj"],
            gain_grad(dense_up, dense_grads["up"], dense_mlp_gain),
            dense_grads["up"],
            dense_grads["down"],
            gain_grad(routed_qkv, routed_grads["qkv"], routed_attn_gain),
            routed_grads["qkv"],
            routed_grads["proj"],
            gain_grad(routed_up, routed_grads["up"], routed_mlp_gain),
            routed_grads["up"],
            routed_grads["down"],
            router_total,
        )

    return per_device


def solution(mesh):
    both = P(("wide", "narrow"))
    wide = P("wide")
    weights = (wide,) * 6
    return jax.shard_map(
        make_device(mesh.shape["wide"], mesh.shape["narrow"]),
        mesh=mesh,
        in_specs=(both, both, both, both) + weights + weights + (P(),),
        out_specs=(both, both) + weights + weights + (P(),),
        check_vma=False,
    )
```

```python
import functools

import jax
import jax.numpy as jnp
from jax import lax
from jax.experimental import pallas as pl
from jax.experimental.pallas import tpu as pltpu
from jax.sharding import PartitionSpec as P

HEADS = 16
EPS = 1e-06
NEG = -1e30
HIGH = lax.Precision.HIGHEST
LOW = jnp.bfloat16
F32 = jnp.float32
I32 = jnp.int32
VMEM_SPEC = pl.BlockSpec(memory_space=pltpu.VMEM)
SMEM_SPEC = pl.BlockSpec(memory_space=pltpu.SMEM)
ANY_SPEC = pl.BlockSpec(memory_space=pl.ANY)


def dot_rows(left, right):
    return jnp.dot(left, right, preferred_element_type=F32)


def dot_cross(left, right):
    return lax.dot_general(left, right, (((0,), (0,)), ((), ())), preferred_element_type=F32)


def dot_back(left, right):
    return lax.dot_general(left, right, (((1,), (1,)), ((), ())), preferred_element_type=F32)


def bits_of(size):
    found = []
    bit = size // 2
    while bit >= 1:
        found.append(bit)
        bit //= 2
    return found


def xor_blocks(array, index, blocks, axis):
    size = array.shape[axis] // blocks
    for bit in bits_of(blocks):
        parts = [
            lax.slice_in_dim(array, k * size, (k + 1) * size, axis=axis) for k in range(blocks)
        ]
        swapped = jnp.concatenate([parts[k ^ bit] for k in range(blocks)], axis=axis)
        array = jnp.where((index & bit) != 0, swapped, array)
    return array


class Links:
    def __init__(self, sizes):
        self.sizes = sizes

    def swap(self, array, axis, bit):
        return lax.ppermute(array, axis, [(i, i ^ bit) for i in range(self.sizes[axis])])

    def gather(self, local, axis, order):
        for bit in order:
            local = jnp.concatenate([local, self.swap(local, axis, bit)], 0)
        return local


class Gather:
    def __init__(self, links, piece, order):
        self.links = links
        self.arrays = [piece]
        self.offsets = [[0]]
        self.todo = [(order[0], None)]
        made = 1
        for bit in order[1:]:
            self.todo += [(bit, i) for i in range(made)]
            made *= 2

    def next(self, count=1):
        for bit, at in self.todo[:count]:
            got = self.links.swap(self.arrays[at or 0], "wide", bit)
            offsets = [k ^ bit for k in self.offsets[at or 0]]
            if at is None:
                self.arrays = [jnp.concatenate([self.arrays[0], got], 0)]
                self.offsets = [self.offsets[0] + offsets]
            else:
                self.arrays.append(got)
                self.offsets.append(offsets)
        self.todo = self.todo[count:]

    def finish(self):
        self.next(len(self.todo))
        return list(zip(self.offsets, self.arrays))


class Scatter:
    def __init__(self, links, columns, index, order):
        self.links = links
        self.index = index
        self.bits = bits_of(links.sizes["wide"])
        self.left = list(order[::-1])
        lead = (2,) * len(self.bits)
        size = links.sizes["wide"]
        self.base = [c.reshape(lead + (c.shape[0] // size, c.shape[1])) for c in columns]
        self.got = None
        self.at = None
        self.mine = None

    @property
    def arrays(self):
        return [self.base] if self.got is None else [self.base, self.got]

    @arrays.setter
    def arrays(self, values):
        self.base = values[0]
        if self.got is not None:
            self.got = values[1]

    def value(self):
        def pick(c):
            return lax.dynamic_index_in_dim(c, self.mine, self.at, keepdims=False)

        if self.got is None:
            return jnp.concatenate(self.base, -1) if len(self.base) > 1 else self.base[0]
        kept = jnp.concatenate([pick(c) for c in self.base], -1)
        return (kept.astype(F32) + self.got.astype(F32)).astype(LOW)

    def next(self):
        if not self.left:
            return
        bit = self.left.pop(0)
        at = self.bits.index(bit)
        mine = jnp.where((self.index & bit) != 0, 1, 0).astype(I32)
        if self.got is not None:
            self.base = [self.value()]
        send = jnp.concatenate(
            [lax.dynamic_index_in_dim(c, 1 - mine, at, keepdims=False) for c in self.base], -1
        )
        self.bits.pop(at)
        self.at, self.mine = at, mine
        self.got = self.links.swap(send, "wide", bit)

    def finish(self):
        while self.left:
            self.next()
        return self.value()


def sync(movers, *values):
    held = lax.optimization_barrier(([m.arrays for m in movers], values))
    for mover, arrays in zip(movers, held[0]):
        mover.arrays = arrays
    return held[1]


def order_of(order):
    offsets = [0]
    for bit in order:
        offsets = offsets + [k ^ bit for k in offsets]
    return offsets


def pack(index, narrow, shards, layouts):
    def kernel(index_ref, *refs):
        ins, outs, sems = refs[: len(shards)], refs[len(shards) : -1], refs[-1]
        at = index_ref[0]
        copies = []

        def add(source, target):
            copies.append(pltpu.make_async_copy(source, target, sems.at[len(copies)]))

        for (out, members), out_ref in zip(layouts, outs):
            low = 0
            for member, blocks, width in members:
                source = ins[member]
                if blocks is None:
                    size = source.shape[0] // narrow
                    add(source.at[pl.ds(pl.multiple_of(at * size, size), size), :], out_ref.at[0])
                    continue
                for block in range(blocks):
                    start = pl.multiple_of((block * narrow + at) * width, width)
                    add(source.at[:, pl.ds(start, width)], out_ref.at[0, :, low : low + width])
                    low += width
        for copy in copies:
            copy.start()
        for copy in copies:
            copy.wait()

    count = sum(1 if m[1] is None else m[1] for _, members in layouts for m in members)
    return pl.pallas_call(
        kernel,
        out_shape=[jax.ShapeDtypeStruct((1,) + shape, LOW) for shape, _ in layouts],
        in_specs=[SMEM_SPEC] + [ANY_SPEC] * len(shards),
        out_specs=[VMEM_SPEC] * len(layouts),
        scratch_shapes=[pltpu.SemaphoreType.DMA((count,))],
    )(index.reshape(1), *shards)


def assemble(parts, index, widths):
    count = sum(len(ks) for ks, _ in parts)
    own = parts[0][1].shape[1]
    spans = []
    start = 0
    for width in widths:
        spans.append((start, start + width))
        start += width

    def kernel(index_ref, *refs):
        ins, outs, sems = refs[: len(parts)], refs[len(parts) : -1], refs[-1]
        copies = []
        for (ks, _), source in zip(parts, ins):
            for j, k in enumerate(ks):
                row = pl.multiple_of((index_ref[0] ^ k) * own, own)
                for (low, high), out in zip(spans, outs):
                    copies.append(
                        pltpu.make_async_copy(
                            source.at[j, :, low:high],
                            out.at[pl.ds(row, own), :],
                            sems.at[len(copies)],
                        )
                    )
        for copy in copies:
            copy.start()
        for copy in copies:
            copy.wait()

    return pl.pallas_call(
        kernel,
        out_shape=[jax.ShapeDtypeStruct((count * own, width), LOW) for width in widths],
        in_specs=[SMEM_SPEC] + [ANY_SPEC] * len(parts),
        out_specs=[VMEM_SPEC] * len(widths),
        scratch_shapes=[pltpu.SemaphoreType.DMA((count * len(widths),))],
    )(index.reshape(1), *[a for _, a in parts])


def head_columns(ref, part, head, heads, width):
    start = (part * heads + head) * width
    return ref[:, start : start + width]


def head_prob(query, key, bias):
    scores = dot_back(query, key) + bias
    lifted = jnp.exp(scores - jnp.max(scores, -1, keepdims=True))
    return lifted / jnp.sum(lifted, -1, keepdims=True)


def attend_kernel(heads, combined_ref, bias_ref, out_ref):
    width = out_ref.shape[1] // heads
    bias = bias_ref[0]
    outs = []
    for head in range(heads):
        query = head_columns(combined_ref, 0, head, heads, width) * LOW(width**-0.5)
        key = head_columns(combined_ref, 1, head, heads, width)
        val = head_columns(combined_ref, 2, head, heads, width)
        prob = head_prob(query, key, bias).astype(LOW)
        outs.append(dot_rows(prob, val).astype(LOW))
    out_ref[...] = jnp.concatenate(outs, 1)


def attend_back_kernel(heads, combined_ref, grad_ref, bias_ref, out_ref):
    width = grad_ref.shape[1] // heads
    scale = width**-0.5
    bias = bias_ref[0]
    outs = [[], [], []]
    for head in range(heads):
        query = head_columns(combined_ref, 0, head, heads, width) * LOW(scale)
        key = head_columns(combined_ref, 1, head, heads, width)
        val = head_columns(combined_ref, 2, head, heads, width)
        grad = head_columns(grad_ref, 0, head, heads, width)
        prob = head_prob(query, key, bias)
        prob_grad = dot_back(grad, val)
        inner = jnp.sum(prob * prob_grad, -1, keepdims=True)
        score_grad = (prob * (prob_grad - inner)).astype(LOW)
        outs[0].append((dot_rows(score_grad, key) * scale).astype(LOW))
        outs[1].append(dot_cross(score_grad, query).astype(LOW))
        outs[2].append(dot_cross(prob.astype(LOW), grad).astype(LOW))
    out_ref[...] = jnp.concatenate(outs[0] + outs[1] + outs[2], 1)


def attend_call(heads, combined, bias, out_grad=None):
    groups, rows, _ = bias.shape
    third = combined.shape[1] // 3

    def rows_spec(cols):
        return pl.BlockSpec((rows, cols), lambda i: (i, 0))

    bias_spec = pl.BlockSpec((1, rows, rows), lambda i: (i, 0, 0))
    total = groups * rows
    if out_grad is None:
        return pl.pallas_call(
            functools.partial(attend_kernel, heads),
            grid=(groups,),
            out_shape=jax.ShapeDtypeStruct((total, third), LOW),
            in_specs=[rows_spec(3 * third), bias_spec],
            out_specs=rows_spec(third),
        )(combined, bias)
    return pl.pallas_call(
        functools.partial(attend_back_kernel, heads),
        grid=(groups,),
        out_shape=jax.ShapeDtypeStruct((total, 3 * third), LOW),
        in_specs=[rows_spec(3 * third), rows_spec(third), bias_spec],
        out_specs=rows_spec(3 * third),
    )(combined, out_grad, bias)


def place(gathered, index, order, plans):
    count, _, own, _ = gathered.shape

    def kernel(index_ref, in_ref, *out_refs):
        for j in range(count):
            offset = index_ref[0] ^ j
            entry = 0
            for position, k in enumerate(order):
                entry = jnp.where(offset == k, position, entry)
            for (group, first, pieces, chunk), out_ref in zip(plans, out_refs):
                if chunk is None:
                    out_ref[j * own : (j + 1) * own, :] = in_ref[entry, group].astype(F32)
                    continue
                for p in range(pieces):
                    at = (p * count + j) * chunk
                    low = first + p * chunk
                    out_ref[:, at : at + chunk] = in_ref[
                        entry, group, :, low : low + chunk
                    ].astype(F32)

    shapes = [
        (count * own, gathered.shape[3]) if chunk is None else (own, pieces * count * chunk)
        for _, _, pieces, chunk in plans
    ]
    return pl.pallas_call(
        kernel,
        out_shape=[jax.ShapeDtypeStruct(shape, F32) for shape in shapes],
        in_specs=[SMEM_SPEC, VMEM_SPEC],
        out_specs=[VMEM_SPEC] * len(plans),
    )(index.reshape(1), gathered)


def norm_stats(values):
    return lax.rsqrt(jnp.mean(values * values, -1, keepdims=True) + EPS)


def norm_back(values, scale, gain, grad):
    weighted = grad * gain
    inner = jnp.mean(weighted * values, -1, keepdims=True)
    return scale * (weighted - values * (scale * scale) * inner)


def gelu_parts(v):
    root = 0.7978845608028654
    inner = jnp.tanh(root * (v + 0.044715 * v * v * v))
    value = 0.5 * v * (1.0 + inner)
    slope = 0.5 * (1.0 + inner) + 0.5 * v * (1.0 - inner * inner) * root * (
        1.0 + 3.0 * 0.044715 * v * v
    )
    return value, slope


def make_device(wide, narrow):
    wide_bits = bits_of(wide)
    narrow_bits = bits_of(narrow)
    order_a = list(wide_bits)
    order_b = wide_bits[:-2] + wide_bits[-2:][::-1]
    near = order_of(narrow_bits)

    def per_device(
        tokens,
        segment_ids,
        routed_index,
        out_grad,
        dense_attn_gain,
        dense_qkv,
        dense_proj,
        dense_mlp_gain,
        dense_up,
        dense_down,
        routed_attn_gain,
        routed_qkv,
        routed_proj,
        routed_mlp_gain,
        routed_up,
        routed_down,
        router_vector,
    ):
        links = Links({"wide": wide, "narrow": narrow})
        w = lax.axis_index("wide").astype(I32)
        n = lax.axis_index("narrow").astype(I32)
        inputs = tokens[0].astype(F32)
        rows, width = inputs.shape
        segments = segment_ids[0]
        chosen = routed_index[0]
        cap = chosen.shape[0]
        heads = HEADS // narrow
        own = width // wide
        ffn = dense_up.shape[1]
        part = width // narrow
        unit = ffn // (wide * narrow)

        def pieces_of(qkv, proj, up, down):
            if unit % 128 == 0:
                return pack(
                    n,
                    narrow,
                    [qkv, proj, up, down],
                    [
                        ((own, 4 * part), [(0, 3, part), (1, 1, part)]),
                        ((own, ffn // narrow), [(2, wide, unit)]),
                        ((unit, width), [(3, None, None)]),
                    ],
                )
            mixed = jnp.concatenate(
                [qkv.reshape(own, 3, narrow, part), proj.reshape(own, 1, narrow, part)], 1
            )

            def pick(array, axis):
                return lax.dynamic_index_in_dim(array, n, axis, keepdims=False)

            return (
                pick(mixed, 2).reshape(1, own, 4 * part),
                pick(up.reshape(own, wide, narrow, unit), 2).reshape(1, own, -1),
                pick(down.reshape(narrow, unit, width), 0)[None],
            )

        def swap_blocks(array, axis):
            got = []
            for k in range(narrow):
                block = lax.dynamic_slice_in_dim(array, (n ^ k) * part, part, axis)
                got.append(block if k == 0 else links.swap(block, "narrow", k))
            return got

        def open_attn(parts):
            qkv_full, proj_cols = assemble(parts, w, (3 * part, part))
            got = swap_blocks(proj_cols, 0)
            return qkv_full, xor_blocks(jnp.concatenate(got, 1), n, narrow, 1)

        def proj_columns(proj_grad):
            return xor_blocks(jnp.concatenate(swap_blocks(proj_grad, 1), 0), n, narrow, 0)

        def flat(array):
            return array.reshape(-1, array.shape[-1])

        def share_far(local):
            return links.gather(local[None], "narrow", narrow_bits[:-1])

        def share_core(first):
            return links.swap(first, "narrow", narrow_bits[-1])

        def share(local):
            first = share_far(local)
            return jnp.concatenate([first, share_core(first)], 0)

        def total_core(first, second):
            got = share_core(second)
            keep = first.reshape(narrow // 2, -1, width)
            return keep.astype(F32) + got.reshape(narrow // 2, -1, width).astype(F32)

        def total_far(sums):
            for bit in narrow_bits[:-1][::-1]:
                half = sums.shape[0] // 2
                got = links.swap(sums[half:].astype(LOW), "narrow", bit)
                sums = sums[:half] + got.astype(F32)
            return sums[0]

        def total(whole):
            half = whole.shape[0] // 2
            return total_far(total_core(whole[:half], whole[half:]))

        def rows_low(chunk, weight):
            return dot_rows(chunk, weight).astype(LOW)

        def back_low(chunk, weight):
            return dot_back(chunk, weight).astype(LOW)

        def cross(lefts, rights):
            out = dot_cross(lefts[0], rights[0])
            for left, right in zip(lefts[1:], rights[1:]):
                out = out + dot_cross(left, right)
            return out.astype(LOW)

        def normed_of(values, scale, gain):
            return (values * scale * gain).astype(LOW)

        def active_of(hidden_pre):
            return gelu_parts(hidden_pre)[0].astype(LOW)

        def pre_grad_of(hidden_pre, grad, down):
            return (gelu_parts(hidden_pre)[1] * dot_back(grad, down)).astype(LOW)

        def gain_grad(weight, grad, gain):
            return jnp.sum(weight.astype(F32) * grad, -1) / gain.astype(F32)

        piece_a, piece_u, piece_d = pieces_of(dense_qkv, dense_proj, dense_up, dense_down)
        get_a = Gather(links, piece_a, order_a)
        get_u = Gather(links, piece_u, order_a)
        get_d = Gather(links, piece_d, order_a)
        get_a.next()
        gains = jnp.stack([dense_attn_gain, dense_mlp_gain, routed_attn_gain, routed_mlp_gain])
        gains = links.gather(gains[None], "wide", order_a)
        marks = share(jnp.concatenate([segments, chosen, jnp.take(segments, chosen)]))
        scale_0 = norm_stats(inputs)
        pieces_r = pieces_of(routed_qkv, routed_proj, routed_up, routed_down)
        full_ra, full_ru, full_rd = [
            lax.all_gather(piece[0], "wide", axis=0, tiled=True) for piece in pieces_r
        ]
        moving = [get_a, get_u, get_d]
        gains, marks, scale_0 = sync(moving, gains, marks, scale_0)

        get_a.next()
        get_u.next()
        spread = order_of(order_a)
        places = jnp.array([spread.index(k) for k in range(wide)], I32)
        gains = jnp.take(gains, places[w ^ jnp.arange(wide, dtype=I32)], axis=0)
        gains = gains.transpose(1, 0, 2).reshape(4, width).astype(F32)
        normed_0 = [share_far(normed_of(inputs, scale_0, gains[0]))]
        gains, normed_0, marks = sync(moving, gains, normed_0, marks)

        get_a.next(2)
        get_u.next()
        get_d.next()
        normed_0.append(share_core(normed_0[0]))
        normed_0 = [flat(c) for c in normed_0]
        seg_all = marks[:, :rows]
        pos_r = marks[:, rows : rows + cap]
        seg_r = marks[:, rows + cap :].reshape(-1)
        where_r, of_r = pos_r.reshape(-1), jnp.repeat(jnp.arange(narrow, dtype=I32), cap)
        pos = jnp.arange(rows, dtype=I32)
        allowed = (pos[None, None, :] <= pos[None, :, None]) & (
            seg_all[:, None, :] == seg_all[:, :, None]
        )
        bias_0 = jnp.where(allowed, 0.0, NEG).astype(F32)
        bias_0 = [bias_0[: narrow // 2], bias_0[narrow // 2 :]]
        allowed = (where_r[None, :] <= where_r[:, None]) & (seg_r[None, :] == seg_r[:, None])
        allowed = allowed & (of_r[None, :] == of_r[:, None])
        bias_r = jnp.where(allowed, 0.0, NEG).astype(F32)[None]
        hits_all = (pos[None, :, None] == pos_r[:, None, :]).astype(LOW)
        normed_0, bias_0 = sync(moving, normed_0, bias_0)

        moving = [get_u, get_d]
        get_u.next(2)
        get_d.next()
        qkv_d, proj_d = open_attn(get_a.finish())
        combined_0 = [rows_low(c, qkv_d) for c in normed_0]
        attended_0 = [attend_call(heads, c, b) for c, b in zip(combined_0, bias_0)]
        second = rows_low(attended_0[1], proj_d)
        sums = total_core(rows_low(attended_0[0], proj_d), second)
        attended_0, proj_d, qkv_d, sums = sync(moving, attended_0, proj_d, qkv_d, sums)

        get_d.next(2)
        hidden = inputs + total_far(sums)
        scale_1 = norm_stats(hidden)
        normed_1 = [share_far(normed_of(hidden, scale_1, gains[1]))]
        up_d = assemble(get_u.finish(), w, (ffn // narrow,))[0]
        normed_1.append(share_core(normed_1[0]))
        normed_1 = [flat(c) for c in normed_1]
        pre_1 = [dot_rows(c, up_d) for c in normed_1]
        active_1 = [active_of(c) for c in pre_1]
        active_1, pre_1, up_d = sync([get_d], active_1, pre_1, up_d)
        down_d = assemble(get_d.finish(), w, (width,))[0]
        second = rows_low(active_1[1], down_d)
        sums = total_core(rows_low(active_1[0], down_d), second)
        middle = hidden + total_far(sums)

        selected = jnp.take(middle, chosen, axis=0)
        route_vec = router_vector.astype(F32)
        rate = jax.nn.sigmoid(jnp.dot(selected, route_vec, precision=HIGH))
        scale_2 = norm_stats(selected)
        normed_2 = flat(share(normed_of(selected, scale_2, gains[2])))
        qkv_r, proj_r = full_ra[:, : 3 * part], swap_blocks(full_ra[:, 3 * part :], 0)
        proj_r = xor_blocks(jnp.concatenate(proj_r, 1), n, narrow, 1)
        combined_2 = rows_low(normed_2, qkv_r)
        attended_2 = attend_call(heads, combined_2, bias_r)
        routed_att = total(rows_low(attended_2, proj_r))
        result_grad = out_grad[0]
        picked_grad = jnp.take(result_grad, chosen, axis=0).astype(F32)
        change_grad = rate[:, None] * picked_grad
        grad_3 = flat(share(change_grad.astype(LOW)))

        scale_3 = norm_stats(selected + routed_att)
        normed_3 = flat(share(normed_of(selected + routed_att, scale_3, gains[3])))
        grad_far = share_far(result_grad)
        grad_share = [grad_far, share_core(grad_far)]
        up_r, down_r = full_ru, full_rd
        pre_3 = dot_rows(normed_3, up_r)
        active_3 = active_of(pre_3)
        routed_out = rows_low(active_3, down_r)

        pre_grad_3 = pre_grad_of(pre_3, grad_3, down_r)
        normed_part = back_low(pre_grad_3, up_r)
        both_r = jnp.concatenate(
            [cross([normed_3], [pre_grad_3]), cross([active_3], [grad_3])], 1
        )
        both_r, normed_part, routed_out, grad_share = sync(
            [], both_r, normed_part, routed_out, grad_share
        )
        shard_r = lax.psum_scatter(both_r, "wide", scatter_dimension=0, tiled=True)

        after = selected + routed_att
        after_grad = norm_back(after, scale_3, gains[3], total(normed_part))
        grad_2 = flat(share((change_grad + after_grad).astype(LOW)))
        combined_grad_2 = attend_call(heads, combined_2, bias_r, back_low(grad_2, proj_r))
        normed_part = back_low(combined_grad_2, qkv_r)
        change = routed_att + total(routed_out)
        normed_part, change, grad_2, combined_grad_2 = sync(
            [], normed_part, change, grad_2, combined_grad_2
        )

        rate_grad = jnp.sum(picked_grad * change, -1)
        logit_grad = rate_grad * rate * (1.0 - rate)
        att_in_grad = norm_back(selected, scale_2, gains[2], total(normed_part))
        selected_grad = after_grad + att_in_grad + logit_grad[:, None] * route_vec[None, :]
        fresh = share((picked_grad + selected_grad).astype(LOW))
        proj_grad = proj_columns(cross([attended_2], [grad_2]))
        qkv_grad = cross([normed_2], [combined_grad_2])
        put_ra = Scatter(links, [qkv_grad, proj_grad], w, order_a)
        router_total = jnp.dot(logit_grad, selected, precision=HIGH)
        hops = [("narrow", bit) for bit in narrow_bits] + [("wide", bit) for bit in wide_bits]

        def hop(value):
            if hops:
                value = value + links.swap(value, *hops.pop(0))
            return value

        router_total = hop(router_total)
        fresh, selected_grad, router_total = sync(
            [put_ra], fresh, selected_grad, router_total
        )

        put_ra.next()
        placed = jnp.einsum("sqk,skd->sqd", hits_all, fresh, preferred_element_type=F32)
        taken = jnp.any(hits_all != 0, -1, keepdims=True)
        half = narrow // 2
        grad_1 = [
            flat(jnp.where(taken[i * half : (i + 1) * half],
                           placed[i * half : (i + 1) * half].astype(LOW), base))
            for i, base in enumerate(grad_share)
        ]
        pre_grad_1 = [pre_grad_of(h, g, down_d) for h, g in zip(pre_1, grad_1)]
        second = back_low(pre_grad_1[1], up_d)
        sums = total_core(back_low(pre_grad_1[0], up_d), second)
        put_d = Scatter(links, [cross(active_1, grad_1)], w, order_a)
        router_total = hop(router_total)
        moving = [put_ra, put_d]
        sums, pre_grad_1, router_total = sync(moving, sums, pre_grad_1, router_total)

        put_d.next()
        put_ra.next()
        hits = (pos[:, None] == chosen[None, :]).astype(F32)
        middle_grad = result_grad.astype(F32) + jnp.dot(hits, selected_grad, precision=HIGH)
        hidden_grad = middle_grad + norm_back(hidden, scale_1, gains[1], total_far(sums))
        put_u = Scatter(links, [cross(normed_1, pre_grad_1)], w, order_a)
        grad_0 = [share_far(hidden_grad.astype(LOW))]
        router_total = hop(router_total)
        moving = [put_ra, put_d, put_u]
        grad_0, hidden_grad, router_total = sync(moving, grad_0, hidden_grad, router_total)

        put_u.next()
        put_d.next()
        put_ra.next()
        grad_0.append(share_core(grad_0[0]))
        grad_0 = [flat(c) for c in grad_0]
        combined_grad_0 = [
            attend_call(heads, c, b, back_low(g, proj_d))
            for c, b, g in zip(combined_0, bias_0, grad_0)
        ]
        second = back_low(combined_grad_0[1], qkv_d)
        sums = total_core(back_low(combined_grad_0[0], qkv_d), second)
        router_total = hop(router_total)
        sums, combined_grad_0, grad_0, router_total = sync(
            moving, sums, combined_grad_0, grad_0, router_total
        )

        put_u.next()
        put_d.next()
        proj_grad = proj_columns(cross(attended_0, grad_0))
        qkv_grad = cross(normed_0, combined_grad_0)
        put_a = Scatter(links, [qkv_grad, proj_grad], w, order_a)
        input_part = norm_back(inputs, scale_0, gains[0], total_far(sums))
        input_total = (hidden_grad + input_part).astype(LOW)
        router_total = hop(router_total)
        moving = [put_ra, put_d, put_u, put_a]
        input_total, router_total = sync(moving, input_total, router_total)

        def far(shards):
            return links.gather(jnp.stack(shards)[None], "narrow", narrow_bits[:-1])

        put_a.next()
        put_u.next()
        added = jnp.dot(hits, rate[:, None] * change, precision=HIGH)
        result = (middle + added).astype(LOW)
        while hops:
            router_total = hop(router_total)
        result, router_total = sync([put_a, put_u, put_d], result, router_total)

        put_a.next()
        far_d = far([put_u.finish(), put_d.finish()])
        (far_d,) = sync([put_a], far_d)

        put_a.next()
        ffn_part = ffn // narrow
        far_r = far([shard_r[:, :ffn_part], shard_r[:, ffn_part:], put_ra.finish()])
        done_d = jnp.concatenate([far_d, share_core(far_d)], 0)
        done_d, far_r = sync([put_a], done_d, far_r)
        done_r = jnp.concatenate([far_r, share_core(far_r)], 0)
        far_a = far([put_a.finish()])
        done_a = jnp.concatenate([far_a, share_core(far_a)], 0)

        plans_f = [(0, 0, wide, unit), (1, 0, 1, None)]

        def plans_a(group):
            return [(group, 0, 3, part), (group, 3 * part, 1, part)]

        out_up_r, out_down_r, out_qkv_r, out_proj_r = place(done_r, n, near, plans_f + plans_a(2))
        out_up, out_down = place(done_d, n, near, plans_f)
        out_qkv, out_proj = place(done_a, n, near, plans_a(0))
        return (
            result[None],
            input_total[None],
            gain_grad(dense_qkv, out_qkv, dense_attn_gain),
            out_qkv,
            out_proj,
            gain_grad(dense_up, out_up, dense_mlp_gain),
            out_up,
            out_down,
            gain_grad(routed_qkv, out_qkv_r, routed_attn_gain),
            out_qkv_r,
            out_proj_r,
            gain_grad(routed_up, out_up_r, routed_mlp_gain),
            out_up_r,
            out_down_r,
            router_total,
        )

    return per_device


def solution(mesh):
    both = P(("wide", "narrow"))
    wide = P("wide")
    weights = (wide,) * 6
    return jax.shard_map(
        make_device(mesh.shape["wide"], mesh.shape["narrow"]),
        mesh=mesh,
        in_specs=(both, both, both, both) + weights + weights + (P(),),
        out_specs=(both, both) + weights + weights + (P(),),
        check_vma=False,
    )
```

```python
import functools

import jax
import jax.numpy as jnp
from jax import lax
from jax.experimental import pallas as pl
from jax.experimental.pallas import tpu as pltpu
from jax.sharding import PartitionSpec as P

HEADS = 16
EPS = 1e-06
NEG = -1e30
HIGH = lax.Precision.HIGHEST
LOW = jnp.bfloat16
F32 = jnp.float32
I32 = jnp.int32
VMEM_SPEC = pl.BlockSpec(memory_space=pltpu.VMEM)
SMEM_SPEC = pl.BlockSpec(memory_space=pltpu.SMEM)
ANY_SPEC = pl.BlockSpec(memory_space=pl.ANY)


def dot_rows(left, right):
    return jnp.dot(left, right, preferred_element_type=F32)


def dot_cross(left, right):
    return lax.dot_general(left, right, (((0,), (0,)), ((), ())), preferred_element_type=F32)


def dot_back(left, right):
    return lax.dot_general(left, right, (((1,), (1,)), ((), ())), preferred_element_type=F32)


def bits_of(size):
    found = []
    bit = size // 2
    while bit >= 1:
        found.append(bit)
        bit //= 2
    return found


def xor_blocks(array, index, blocks, axis):
    size = array.shape[axis] // blocks
    for bit in bits_of(blocks):
        parts = [
            lax.slice_in_dim(array, k * size, (k + 1) * size, axis=axis) for k in range(blocks)
        ]
        swapped = jnp.concatenate([parts[k ^ bit] for k in range(blocks)], axis=axis)
        array = jnp.where((index & bit) != 0, swapped, array)
    return array


class Links:
    def __init__(self, sizes):
        self.sizes = sizes

    def swap(self, array, axis, bit):
        return lax.ppermute(array, axis, [(i, i ^ bit) for i in range(self.sizes[axis])])

    def gather(self, local, axis, order):
        for bit in order:
            local = jnp.concatenate([local, self.swap(local, axis, bit)], 0)
        return local


class Gather:
    def __init__(self, links, piece, order):
        self.links = links
        self.arrays = [piece]
        self.offsets = [[0]]
        self.todo = [(order[0], None)]
        made = 1
        for bit in order[1:]:
            self.todo += [(bit, i) for i in range(made)]
            made *= 2

    def next(self, count=1):
        for bit, at in self.todo[:count]:
            got = self.links.swap(self.arrays[at or 0], "wide", bit)
            offsets = [k ^ bit for k in self.offsets[at or 0]]
            if at is None:
                self.arrays = [jnp.concatenate([self.arrays[0], got], 0)]
                self.offsets = [self.offsets[0] + offsets]
            else:
                self.arrays.append(got)
                self.offsets.append(offsets)
        self.todo = self.todo[count:]

    def finish(self):
        self.next(len(self.todo))
        return list(zip(self.offsets, self.arrays))


class Scatter:
    def __init__(self, links, columns, index, order):
        self.links = links
        self.index = index
        self.bits = bits_of(links.sizes["wide"])
        self.left = list(order[::-1])
        lead = (2,) * len(self.bits)
        size = links.sizes["wide"]
        self.base = [c.reshape(lead + (c.shape[0] // size, c.shape[1])) for c in columns]
        self.got = None
        self.at = None
        self.mine = None

    @property
    def arrays(self):
        return [self.base] if self.got is None else [self.base, self.got]

    @arrays.setter
    def arrays(self, values):
        self.base = values[0]
        if self.got is not None:
            self.got = values[1]

    def value(self):
        def pick(c):
            return lax.dynamic_index_in_dim(c, self.mine, self.at, keepdims=False)

        if self.got is None:
            return jnp.concatenate(self.base, -1) if len(self.base) > 1 else self.base[0]
        kept = jnp.concatenate([pick(c) for c in self.base], -1)
        return (kept.astype(F32) + self.got.astype(F32)).astype(LOW)

    def next(self):
        if not self.left:
            return
        bit = self.left.pop(0)
        at = self.bits.index(bit)
        mine = jnp.where((self.index & bit) != 0, 1, 0).astype(I32)
        if self.got is not None:
            self.base = [self.value()]
        send = jnp.concatenate(
            [lax.dynamic_index_in_dim(c, 1 - mine, at, keepdims=False) for c in self.base], -1
        )
        self.bits.pop(at)
        self.at, self.mine = at, mine
        self.got = self.links.swap(send, "wide", bit)

    def finish(self):
        while self.left:
            self.next()
        return self.value()


def sync(movers, *values):
    held = lax.optimization_barrier(([m.arrays for m in movers], values))
    for mover, arrays in zip(movers, held[0]):
        mover.arrays = arrays
    return held[1]


def order_of(order):
    offsets = [0]
    for bit in order:
        offsets = offsets + [k ^ bit for k in offsets]
    return offsets


def pack(index, narrow, shards, layouts):
    def kernel(index_ref, *refs):
        ins, outs, sems = refs[: len(shards)], refs[len(shards) : -1], refs[-1]
        at = index_ref[0]
        copies = []

        def add(source, target):
            copies.append(pltpu.make_async_copy(source, target, sems.at[len(copies)]))

        for (out, members), out_ref in zip(layouts, outs):
            low = 0
            for member, blocks, width in members:
                source = ins[member]
                if blocks is None:
                    size = source.shape[0] // narrow
                    row = pl.multiple_of(at * size, size)
                    cols = source.shape[1]
                    add(source.at[pl.ds(row, size), :], out_ref.at[0, :, low : low + cols])
                    low += cols
                    continue
                for block in range(blocks):
                    start = pl.multiple_of((block * narrow + at) * width, width)
                    add(source.at[:, pl.ds(start, width)], out_ref.at[0, :, low : low + width])
                    low += width
        for copy in copies:
            copy.start()
        for copy in copies:
            copy.wait()

    count = sum(1 if m[1] is None else m[1] for _, members in layouts for m in members)
    return pl.pallas_call(
        kernel,
        out_shape=[jax.ShapeDtypeStruct((1,) + shape, LOW) for shape, _ in layouts],
        in_specs=[SMEM_SPEC] + [ANY_SPEC] * len(shards),
        out_specs=[VMEM_SPEC] * len(layouts),
        scratch_shapes=[pltpu.SemaphoreType.DMA((count,))],
    )(index.reshape(1), *shards)


def assemble(sources, index, widths):
    own = sources[0][0][0][1].shape[1]
    arrays = [array for parts, _ in sources for _, array in parts]
    rows = sum(len(ks) for ks, _ in sources[0][0]) * own
    count = sum(len(ks) * len(spans) for parts, spans in sources for ks, _ in parts)

    def kernel(index_ref, *refs):
        ins, outs, sems = refs[: len(arrays)], refs[len(arrays) : -1], refs[-1]
        copies = []
        at_ref = 0
        for parts, spans in sources:
            for ks, _ in parts:
                for j, k in enumerate(ks):
                    row = pl.multiple_of((index_ref[0] ^ k) * own, own)
                    for low, high, out, at in spans:
                        copies.append(
                            pltpu.make_async_copy(
                                ins[at_ref].at[j, :, low:high],
                                outs[out].at[pl.ds(row, own), at : at + high - low],
                                sems.at[len(copies)],
                            )
                        )
                at_ref += 1
        for copy in copies:
            copy.start()
        for copy in copies:
            copy.wait()

    return pl.pallas_call(
        kernel,
        out_shape=[jax.ShapeDtypeStruct((rows, width), LOW) for width in widths],
        in_specs=[SMEM_SPEC] + [ANY_SPEC] * len(arrays),
        out_specs=[VMEM_SPEC] * len(widths),
        scratch_shapes=[pltpu.SemaphoreType.DMA((count,))],
    )(index.reshape(1), *arrays)


def head_columns(ref, part, head, heads, width):
    start = (part * heads + head) * width
    return ref[:, start : start + width]


def head_prob(query, key, bias):
    scores = dot_back(query, key) + bias
    lifted = jnp.exp(scores - jnp.max(scores, -1, keepdims=True))
    return lifted / jnp.sum(lifted, -1, keepdims=True)


def write_part(part_refs, value):
    for i, ref in enumerate(part_refs):

        @pl.when(pl.program_id(0) == i)
        def _():
            ref[...] = value


def attend_kernel(
    heads, normed_ref, qkv_ref, proj_ref, bias_ref, combined_ref, out_ref, *part_refs
):
    width = out_ref.shape[1] // heads
    bias = bias_ref[0]
    combined_ref[...] = dot_rows(normed_ref[...], qkv_ref[...]).astype(LOW)
    outs = []
    for head in range(heads):
        query = head_columns(combined_ref, 0, head, heads, width) * LOW(width**-0.5)
        key = head_columns(combined_ref, 1, head, heads, width)
        val = head_columns(combined_ref, 2, head, heads, width)
        prob = head_prob(query, key, bias).astype(LOW)
        outs.append(dot_rows(prob, val).astype(LOW))
    attended = jnp.concatenate(outs, 1)
    out_ref[...] = attended
    write_part(part_refs, dot_rows(attended, proj_ref[...]).astype(LOW))


def attend_back_kernel(
    heads, grad_ref, qkv_ref, proj_ref, bias_ref, combined_ref, out_ref, *rest
):
    part_refs, low_ref = rest[:-1], rest[-1]
    width = low_ref.shape[1] // heads
    scale = width**-0.5
    bias = bias_ref[0]
    low_ref[...] = dot_back(grad_ref[...], proj_ref[...]).astype(LOW)
    outs = [[], [], []]
    for head in range(heads):
        query = head_columns(combined_ref, 0, head, heads, width) * LOW(scale)
        key = head_columns(combined_ref, 1, head, heads, width)
        val = head_columns(combined_ref, 2, head, heads, width)
        grad = head_columns(low_ref, 0, head, heads, width)
        prob = head_prob(query, key, bias)
        prob_grad = dot_back(grad, val)
        inner = jnp.sum(prob * prob_grad, -1, keepdims=True)
        score_grad = (prob * (prob_grad - inner)).astype(LOW)
        outs[0].append((dot_rows(score_grad, key) * scale).astype(LOW))
        outs[1].append(dot_cross(score_grad, query).astype(LOW))
        outs[2].append(dot_cross(prob.astype(LOW), grad).astype(LOW))
    combined_grad = jnp.concatenate(outs[0] + outs[1] + outs[2], 1)
    out_ref[...] = combined_grad
    write_part(part_refs, dot_back(combined_grad, qkv_ref[...]).astype(LOW))


def attend_call(heads, values, qkv, proj, bias, combined=None):
    groups, rows, _ = bias.shape
    width = values.shape[1]
    third = proj.shape[0]
    total = groups * rows

    def rows_spec(cols):
        return pl.BlockSpec((rows, cols), lambda i: (i, 0))

    def whole_spec(array):
        return pl.BlockSpec(array.shape, lambda i: (0, 0))

    bias_spec = pl.BlockSpec((1, rows, rows), lambda i: (i, 0, 0))
    in_specs = [rows_spec(width), whole_spec(qkv), whole_spec(proj), bias_spec]
    wide_out = jax.ShapeDtypeStruct((total, 3 * third), LOW)
    part_outs = [jax.ShapeDtypeStruct((rows, width), LOW)] * groups
    part_specs = [pl.BlockSpec((rows, width), lambda i: (0, 0))] * groups
    if combined is None:
        return pl.pallas_call(
            functools.partial(attend_kernel, heads),
            grid=(groups,),
            out_shape=[wide_out, jax.ShapeDtypeStruct((total, third), LOW)] + part_outs,
            in_specs=in_specs,
            out_specs=[rows_spec(3 * third), rows_spec(third)] + part_specs,
        )(values, qkv, proj, bias)
    return pl.pallas_call(
        functools.partial(attend_back_kernel, heads),
        grid=(groups,),
        out_shape=[wide_out] + part_outs,
        in_specs=in_specs + [rows_spec(3 * third)],
        out_specs=[rows_spec(3 * third)] + part_specs,
        scratch_shapes=[pltpu.VMEM((rows, third), LOW)],
    )(values, qkv, proj, bias, combined)


def tile_call(body, outs, tiled, whole):
    rows = tiled[0].shape[0]
    block = min(rows, 128)
    count = len(tiled) + len(whole)

    def kernel(*refs):
        results = body(*[ref[...] for ref in refs[:count]])
        for ref, result in zip(refs[count:], results):
            ref[...] = result

    def rows_spec(cols):
        return pl.BlockSpec((block, cols), lambda i: (i, 0))

    return pl.pallas_call(
        kernel,
        grid=(rows // block,),
        out_shape=[jax.ShapeDtypeStruct((rows, cols), dtype) for cols, dtype in outs],
        in_specs=[rows_spec(t.shape[1]) for t in tiled]
        + [pl.BlockSpec(t.shape, lambda i: (0, 0)) for t in whole],
        out_specs=[rows_spec(cols) for cols, _ in outs],
    )(*tiled, *whole)


def cross(lefts, rights):
    out = dot_cross(lefts[0], rights[0])
    for left, right in zip(lefts[1:], rights[1:]):
        out = out + dot_cross(left, right)
    return out.astype(LOW)


def place(gathered, index, order, plans):
    count, _, own, _ = gathered.shape

    def kernel(index_ref, in_ref, *out_refs):
        for j in range(count):
            offset = index_ref[0] ^ j
            entry = 0
            for position, k in enumerate(order):
                entry = jnp.where(offset == k, position, entry)
            for (group, first, pieces, chunk), out_ref in zip(plans, out_refs):
                if chunk is None:
                    out_ref[j * own : (j + 1) * own, :] = in_ref[entry, group].astype(F32)
                    continue
                for p in range(pieces):
                    at = (p * count + j) * chunk
                    low = first + p * chunk
                    out_ref[:, at : at + chunk] = in_ref[
                        entry, group, :, low : low + chunk
                    ].astype(F32)

    shapes = [
        (count * own, gathered.shape[3]) if chunk is None else (own, pieces * count * chunk)
        for _, _, pieces, chunk in plans
    ]
    return pl.pallas_call(
        kernel,
        out_shape=[jax.ShapeDtypeStruct(shape, F32) for shape in shapes],
        in_specs=[SMEM_SPEC, VMEM_SPEC],
        out_specs=[VMEM_SPEC] * len(plans),
    )(index.reshape(1), gathered)


def norm_stats(values):
    return lax.rsqrt(jnp.mean(values * values, -1, keepdims=True) + EPS)


def norm_back(values, scale, gain, grad):
    weighted = grad * gain
    inner = jnp.mean(weighted * values, -1, keepdims=True)
    return scale * (weighted - values * (scale * scale) * inner)


def gelu_parts(v):
    root = 0.7978845608028654
    inner = jnp.tanh(root * (v + 0.044715 * v * v * v))
    value = 0.5 * v * (1.0 + inner)
    slope = 0.5 * (1.0 + inner) + 0.5 * v * (1.0 - inner * inner) * root * (
        1.0 + 3.0 * 0.044715 * v * v
    )
    return value, slope


def make_device(wide, narrow):
    wide_bits = bits_of(wide)
    narrow_bits = bits_of(narrow)
    order_a = list(wide_bits)
    order_c = wide_bits[-1:] + wide_bits[:-1]
    near_order = order_of(narrow_bits)

    def per_device(
        tokens,
        segment_ids,
        routed_index,
        out_grad,
        dense_attn_gain,
        dense_qkv,
        dense_proj,
        dense_mlp_gain,
        dense_up,
        dense_down,
        routed_attn_gain,
        routed_qkv,
        routed_proj,
        routed_mlp_gain,
        routed_up,
        routed_down,
        router_vector,
    ):
        links = Links({"wide": wide, "narrow": narrow})
        w = lax.axis_index("wide").astype(I32)
        n = lax.axis_index("narrow").astype(I32)
        inputs = tokens[0].astype(F32)
        rows, width = inputs.shape
        segments = segment_ids[0]
        chosen = routed_index[0]
        cap = chosen.shape[0]
        heads = HEADS // narrow
        own = width // wide
        ffn = dense_up.shape[1]
        part = width // narrow
        unit = ffn // (wide * narrow)

        def pack_some(shards, kinds):
            def up_of(member):
                shard = shards[member].reshape(own, wide, narrow, unit)
                piece = lax.dynamic_index_in_dim(shard, n, 2, keepdims=False)
                return piece.reshape(own, ffn // narrow)

            def down_of(member):
                shard = shards[member].reshape(narrow, unit, width)
                return lax.dynamic_index_in_dim(shard, n, 0, keepdims=False)

            def attn_of(member):
                mixed = jnp.concatenate([shards[member], shards[member + 1]], 1)
                mixed = mixed.reshape(own, 4, narrow, part)
                piece = lax.dynamic_index_in_dim(mixed, n, 2, keepdims=False)
                return piece.reshape(own, 4 * part)

            layouts, pieces, member = [], [], 0
            for kind in kinds:
                if kind == "a":
                    members = [(member, 3, part), (member + 1, 1, part)]
                    layouts.append(((own, 4 * part), members))
                    pieces.append(lambda m=member: attn_of(m))
                elif kind == "u":
                    layouts.append(((own, ffn // narrow), [(member, wide, unit)]))
                    pieces.append(lambda m=member: up_of(m))
                else:
                    layouts.append(((unit, width), [(member, None, None)]))
                    pieces.append(lambda m=member: down_of(m))
                member += 2 if kind == "a" else 1
            if unit % 128 == 0:
                return pack(n, narrow, shards, layouts)
            return [piece()[None] for piece in pieces]

        def swap_blocks(array, axis):
            got = []
            for k in range(narrow):
                block = lax.dynamic_slice_in_dim(array, (n ^ k) * part, part, axis)
                got.append(block if k == 0 else links.swap(block, "narrow", k))
            return got

        def open_proj(proj_cols):
            return xor_blocks(jnp.concatenate(swap_blocks(proj_cols, 0), 1), n, narrow, 1)

        def open_rows(parts, columns):
            return assemble([(parts, [(0, columns, 0, 0)])], w, (columns,))[0]

        def proj_columns(proj_grad):
            return xor_blocks(jnp.concatenate(swap_blocks(proj_grad, 1), 0), n, narrow, 0)

        def flat(array):
            return array.reshape(-1, array.shape[-1])

        def share_core(local):
            return jnp.concatenate([local, links.swap(local, "narrow", 1)], 0)

        def swap_far(local):
            return links.swap(local, "narrow", 2)

        def share(local):
            got = [local] + [links.swap(local, "narrow", k) for k in range(1, narrow)]
            return jnp.stack(got, 0)

        def total(whole):
            parts = whole.reshape(narrow, -1, width)
            out = parts[0].astype(F32)
            for k in range(1, narrow):
                out = out + links.swap(parts[k], "narrow", k).astype(F32)
            return out

        def total_core(keep, send):
            return keep.astype(F32) + links.swap(send, "narrow", 1).astype(F32)

        def total_far(keep, send):
            return swap_far(total_core(keep, send).astype(LOW))

        def halves(chunk):
            half = chunk.shape[0] // 2
            return chunk[:half], chunk[half:]

        def normed_of(values, scale, gain):
            return (values * scale * gain).astype(LOW)

        def up_body(normed, up):
            pre = dot_rows(normed, up)
            return pre, gelu_parts(pre)[0].astype(LOW)

        def both_body(normed, grad, up, down):
            pre = dot_rows(normed, up)
            value, slope = gelu_parts(pre)
            active = value.astype(LOW)
            pre_grad = (slope * dot_back(grad, down)).astype(LOW)
            part = dot_back(pre_grad, up).astype(LOW)
            return active, dot_rows(active, down).astype(LOW), pre_grad, part

        def gain_grad(weight, grad, gain):
            return jnp.sum(weight.astype(F32) * grad, -1) / gain.astype(F32)

        unit_all = ffn // narrow

        (piece_a,) = pack_some([dense_qkv, dense_proj], "a")
        split = 2 * part
        get_a = Gather(links, piece_a[:, :, :split], order_a)
        get_b = Gather(links, piece_a[:, :, split:], order_c)
        get_a.next()
        get_b.next()
        gains = jnp.stack([dense_attn_gain, dense_mlp_gain, routed_attn_gain, routed_mlp_gain])
        gains = links.gather(gains[None], "wide", order_a[:1])
        (gains,) = sync([get_a, get_b], gains)

        get_a.next(2)
        get_b.next()
        gains = links.gather(gains, "wide", order_a[1:])
        marks = share(jnp.concatenate([segments, chosen, jnp.take(segments, chosen)]))
        scale_0 = norm_stats(inputs)
        piece_u, piece_d, *pieces_r = pack_some(
            [dense_up, dense_down, routed_qkv, routed_proj, routed_up, routed_down], "udaud"
        )
        get_u = Gather(links, piece_u, order_a)
        get_d = Gather(links, piece_d, order_a)
        everything = [get_a, get_b, get_u, get_d]
        gains, scale_0, marks = sync(everything, gains, scale_0, marks)

        get_a.next()
        get_b.next(2)
        get_u.next()
        spread = order_of(order_a)
        places = jnp.array([spread.index(k) for k in range(wide)], I32)
        gains = jnp.take(gains, places[w ^ jnp.arange(wide, dtype=I32)], axis=0)
        gains = gains.transpose(1, 0, 2).reshape(4, width).astype(F32)
        normed = normed_of(inputs, scale_0, gains[0])
        far = swap_far(normed)
        normed_0 = [share_core(normed)]
        seg_all = marks[:, :rows]
        pos_r = marks[:, rows : rows + cap]
        seg_r = marks[:, rows + cap :].reshape(-1)
        where_r, of_r = pos_r.reshape(-1), jnp.repeat(jnp.arange(narrow, dtype=I32), cap)
        pos = jnp.arange(rows, dtype=I32)
        allowed = (pos[None, None, :] <= pos[None, :, None]) & (
            seg_all[:, None, :] == seg_all[:, :, None]
        )
        bias_0 = jnp.where(allowed, 0.0, NEG).astype(F32)
        bias_0 = [bias_0[: narrow // 2], bias_0[narrow // 2 :]]
        allowed = (where_r[None, :] <= where_r[:, None]) & (seg_r[None, :] == seg_r[:, None])
        allowed = allowed & (of_r[None, :] == of_r[:, None])
        bias_r = jnp.where(allowed, 0.0, NEG).astype(F32)[None]
        hits_all = (pos[None, :, None] == pos_r[:, None, :]).astype(LOW)
        gains, far, normed_0, bias_0, bias_r, hits_all, pieces_r = sync(
            everything, gains, far, normed_0, bias_0, bias_r, hits_all, pieces_r
        )
        full_ra, up_r, down_r = [
            lax.all_gather(piece[0], "wide", axis=0, tiled=True) for piece in pieces_r
        ]

        get_u.next(2)
        normed_0.append(share_core(far))
        qkv_d, proj_d = assemble(
            [
                (get_a.finish(), [(0, split, 0, 0)]),
                (get_b.finish(), [(0, part, 0, split), (part, 2 * part, 1, 0)]),
            ],
            w,
            (3 * part, part),
        )
        proj_d = open_proj(proj_d)
        second = attend_call(heads, normed_0[1], qkv_d, proj_d, bias_0[1])
        everything = [get_u, get_d]
        second, qkv_d, proj_d = sync(everything, second, qkv_d, proj_d)

        get_u.next()
        get_d.next()
        far = total_far(*second[2:])
        first = attend_call(heads, normed_0[0], qkv_d, proj_d, bias_0[0])
        combined_0 = [first[0], second[0]]
        attended_0 = [first[1], second[1]]
        near = total_core(*first[2:])
        near, far = sync(everything, near, far)

        get_d.next(2)
        hidden = inputs + near + far.astype(F32)
        scale_1 = norm_stats(hidden)
        normed = normed_of(hidden, scale_1, gains[1])
        far = swap_far(normed)
        normed_1 = [share_core(normed)]
        up_d = open_rows(get_u.finish(), unit_all)
        everything = everything[1:]
        first = tile_call(up_body, [(unit_all, F32), (unit_all, LOW)], normed_1, [up_d])
        first, far, up_d, hidden, scale_1 = sync(everything, first, far, up_d, hidden, scale_1)

        get_d.next()
        normed_1.append(share_core(far))
        second = tile_call(up_body, [(unit_all, F32), (unit_all, LOW)], [normed_1[1]], [up_d])
        pre_1 = [first[0], second[0]]
        active_1 = [first[1], second[1]]
        active_1, pre_1 = sync(everything, active_1, pre_1)

        down_d = open_rows(get_d.finish(), width)
        far = total_far(*[dot_rows(a, down_d).astype(LOW) for a in halves(active_1[1])])
        near = total_core(*[dot_rows(a, down_d).astype(LOW) for a in halves(active_1[0])])
        near, far, down_d = sync([], near, far, down_d)

        middle = hidden + near + far.astype(F32)
        selected = jnp.take(middle, chosen, axis=0)
        route_vec = router_vector.astype(F32)
        rate = jax.nn.sigmoid(jnp.dot(selected, route_vec, precision=HIGH))
        result_grad = out_grad[0]
        picked_grad = jnp.take(result_grad, chosen, axis=0).astype(F32)
        change_grad = rate[:, None] * picked_grad
        scale_2 = norm_stats(selected)
        normed_2 = flat(share(normed_of(selected, scale_2, gains[2])))
        qkv_r, proj_r = full_ra[:, : 3 * part], open_proj(full_ra[:, 3 * part :])
        combined_2, attended_2, part_2 = attend_call(heads, normed_2, qkv_r, proj_r, bias_r)
        routed_att = total(part_2)
        grad_3 = flat(share(change_grad.astype(LOW)))
        after = selected + routed_att
        scale_3 = norm_stats(after)
        normed_3 = flat(share(normed_of(after, scale_3, gains[3])))
        grad_1 = [share_core(result_grad), share_core(swap_far(result_grad))]

        active_3, routed_out, pre_grad_3, normed_part = tile_call(
            both_body,
            [(unit_all, LOW), (width, LOW), (unit_all, LOW), (width, LOW)],
            [normed_3, grad_3],
            [up_r, down_r],
        )
        both_r = jnp.concatenate(
            [cross([normed_3], [pre_grad_3]), cross([active_3], [grad_3])], 1
        )
        both_r, normed_part, routed_out, grad_1 = sync(
            [], both_r, normed_part, routed_out, grad_1
        )
        shard_r = lax.psum_scatter(both_r, "wide", scatter_dimension=0, tiled=True)

        after_grad = norm_back(after, scale_3, gains[3], total(normed_part))
        grad_2 = flat(share((change_grad + after_grad).astype(LOW)))
        proj_grad = proj_columns(cross([attended_2], [grad_2]))
        combined_grad_2, part_2 = attend_call(heads, grad_2, qkv_r, proj_r, bias_r, combined_2)
        change = routed_att + total(routed_out)
        put_ra = Scatter(links, [cross([normed_2], [combined_grad_2]), proj_grad], w, order_a)
        part_2, change = sync([put_ra], part_2, change)

        put_ra.next()
        rate_grad = jnp.sum(picked_grad * change, -1)
        logit_grad = rate_grad * rate * (1.0 - rate)
        att_in_grad = norm_back(selected, scale_2, gains[2], total(part_2))
        selected_grad = after_grad + att_in_grad + logit_grad[:, None] * route_vec[None, :]
        fresh = share((picked_grad + selected_grad).astype(LOW))
        router_total = jnp.dot(logit_grad, selected, precision=HIGH)
        hops = [("wide", bit) for bit in wide_bits[:-1]]
        hops += [("narrow", bit) for bit in narrow_bits[::-1]] + [("wide", wide_bits[-1])]

        def hop(value):
            if hops:
                value = value + links.swap(value, *hops.pop(0))
            return value

        router_total = hop(router_total)
        placed = jnp.einsum("sqk,skd->sqd", hits_all, fresh, preferred_element_type=F32)
        taken = jnp.any(hits_all != 0, -1, keepdims=True)
        half = narrow // 2
        grad_1 = [
            flat(jnp.where(taken[i * half : (i + 1) * half],
                           placed[i * half : (i + 1) * half].astype(LOW),
                           base.reshape(half, rows, width)))
            for i, base in enumerate(grad_1)
        ]
        put_d = Scatter(links, [cross(active_1, grad_1)], w, order_a)
        grad_1, selected_grad, router_total = sync([put_d], grad_1, selected_grad, router_total)

        put_d.next()

        def back_ffn(i):
            grad = dot_back(grad_1[i], down_d)
            pre_grad = (gelu_parts(pre_1[i])[1] * grad).astype(LOW)
            return pre_grad, dot_back(pre_grad, up_d).astype(LOW)

        second = back_ffn(1)
        far = total_far(*halves(second[1]))
        first = back_ffn(0)
        near = total_core(*halves(first[1]))
        pre_grad_1 = [first[0], second[0]]
        put_u = Scatter(links, [cross(normed_1, pre_grad_1)], w, order_a)
        router_total = hop(router_total)
        near, far, router_total = sync([put_u], near, far, router_total)

        put_u.next()
        hits = (pos[:, None] == chosen[None, :]).astype(F32)
        middle_grad = result_grad.astype(F32) + jnp.dot(hits, selected_grad, precision=HIGH)
        hidden_grad = middle_grad + norm_back(
            hidden, scale_1, gains[1], near + far.astype(F32)
        )
        hidden_low = hidden_grad.astype(LOW)
        far = swap_far(hidden_low)
        grad_0 = [share_core(hidden_low)]
        first = attend_call(heads, grad_0[0], qkv_d, proj_d, bias_0[0], combined_0[0])
        router_total = hop(router_total)
        moving = [put_ra, put_d]
        first, far, hidden_grad, router_total = sync(
            moving, first, far, hidden_grad, router_total
        )

        def around(shards):
            gathered = links.gather(jnp.stack(shards)[None], "narrow", narrow_bits[:-1])
            return links.gather(gathered, "narrow", narrow_bits[-1:])

        put_d.next()
        put_ra.next()
        grad_0.append(share_core(far))
        second = attend_call(heads, grad_0[1], qkv_d, proj_d, bias_0[1], combined_0[1])
        proj_grad = proj_columns(cross(attended_0, grad_0))
        combined_grad_0 = [first[0], second[0]]
        put_a = Scatter(links, [cross(normed_0, combined_grad_0), proj_grad], w, order_a)
        router_total = hop(router_total)
        moving = [put_ra, put_d, put_u, put_a]
        first, second, router_total = sync(moving, first[1:], second[1:], router_total)

        put_a.next()
        put_u.next()
        put_d.next()
        put_ra.next()
        far = total_far(*second)
        near = total_core(*first)
        done_rf = around([shard_r[:, :unit_all], shard_r[:, unit_all:]])
        plans_f = [(0, 0, wide, unit), (1, 0, 1, None)]
        plans_a = [(0, 0, 3, part), (0, 3 * part, 1, part)]
        input_part = norm_back(inputs, scale_0, gains[0], near + far.astype(F32))
        input_total = (hidden_grad + input_part).astype(LOW)
        added = jnp.dot(hits, rate[:, None] * change, precision=HIGH)
        result = (middle + added).astype(LOW)
        moving = [put_ra, put_d, put_u, put_a]
        input_total, result, router_total = sync(moving, input_total, result, router_total)

        put_a.next()
        put_u.next()
        while hops:
            router_total = hop(router_total)
        done_ra = around([put_ra.finish()])
        done_dd = around([put_d.finish()])
        out_up_r, out_down_r = place(done_rf, n, near_order, plans_f)
        gain_ru = gain_grad(routed_up, out_up_r, routed_mlp_gain)
        (gain_ru,) = sync([put_a, put_u], gain_ru)

        put_a.next()
        done_du = around([put_u.finish()])
        out_qkv_r, out_proj_r = place(done_ra, n, near_order, plans_a)
        gain_ra = gain_grad(routed_qkv, out_qkv_r, routed_attn_gain)
        (out_down,) = place(done_dd, n, near_order, [(0, 0, 1, None)])
        out_down, gain_ra = sync([put_a], out_down, gain_ra)

        done_a = around([put_a.finish()])
        (out_up,) = place(done_du, n, near_order, [(0, 0, wide, unit)])
        gain_u = gain_grad(dense_up, out_up, dense_mlp_gain)
        done_a, gain_u = sync([], done_a, gain_u)
        out_qkv, out_proj = place(done_a, n, near_order, plans_a)
        return (
            result[None],
            input_total[None],
            gain_grad(dense_qkv, out_qkv, dense_attn_gain),
            out_qkv,
            out_proj,
            gain_u,
            out_up,
            out_down,
            gain_ra,
            out_qkv_r,
            out_proj_r,
            gain_ru,
            out_up_r,
            out_down_r,
            router_total,
        )

    return per_device


def solution(mesh):
    both = P(("wide", "narrow"))
    wide = P("wide")
    weights = (wide,) * 6
    return jax.shard_map(
        make_device(mesh.shape["wide"], mesh.shape["narrow"]),
        mesh=mesh,
        in_specs=(both, both, both, both) + weights + weights + (P(),),
        out_specs=(both, both) + weights + weights + (P(),),
        check_vma=False,
    )
```

```python
import functools

import jax
import jax.numpy as jnp
from jax import lax
from jax.experimental import pallas as pl
from jax.experimental.pallas import tpu as pltpu
from jax.sharding import PartitionSpec as P

HEADS = 16
EPS = 1e-06
NEG = -1e30
HIGH = lax.Precision.HIGHEST
LOW = jnp.bfloat16
F32 = jnp.float32
I32 = jnp.int32
VMEM_SPEC = pl.BlockSpec(memory_space=pltpu.VMEM)
SMEM_SPEC = pl.BlockSpec(memory_space=pltpu.SMEM)
ANY_SPEC = pl.BlockSpec(memory_space=pl.ANY)


def dot_rows(left, right):
    return jnp.dot(left, right, preferred_element_type=F32)


def dot_cross(left, right):
    return lax.dot_general(left, right, (((0,), (0,)), ((), ())), preferred_element_type=F32)


def dot_back(left, right):
    return lax.dot_general(left, right, (((1,), (1,)), ((), ())), preferred_element_type=F32)


def bits_of(size):
    found = []
    bit = size // 2
    while bit >= 1:
        found.append(bit)
        bit //= 2
    return found


def xor_blocks(array, index, blocks, axis):
    size = array.shape[axis] // blocks
    for bit in bits_of(blocks):
        parts = [
            lax.slice_in_dim(array, k * size, (k + 1) * size, axis=axis) for k in range(blocks)
        ]
        swapped = jnp.concatenate([parts[k ^ bit] for k in range(blocks)], axis=axis)
        array = jnp.where((index & bit) != 0, swapped, array)
    return array


class Links:
    def __init__(self, sizes):
        self.sizes = sizes

    def swap(self, array, axis, bit):
        return lax.ppermute(array, axis, [(i, i ^ bit) for i in range(self.sizes[axis])])

    def gather(self, local, axis, order):
        for bit in order:
            local = jnp.concatenate([local, self.swap(local, axis, bit)], 0)
        return local


class Gather:
    def __init__(self, links, piece, order):
        self.links = links
        self.arrays = [piece]
        self.offsets = [[0]]
        self.todo = [(order[0], None)]
        made = 1
        for bit in order[1:]:
            self.todo += [(bit, i) for i in range(made)]
            made *= 2

    def next(self, count=1):
        for bit, at in self.todo[:count]:
            got = self.links.swap(self.arrays[at or 0], "wide", bit)
            offsets = [k ^ bit for k in self.offsets[at or 0]]
            if at is None:
                self.arrays = [jnp.concatenate([self.arrays[0], got], 0)]
                self.offsets = [self.offsets[0] + offsets]
            else:
                self.arrays.append(got)
                self.offsets.append(offsets)
        self.todo = self.todo[count:]

    def finish(self):
        self.next(len(self.todo))
        return list(zip(self.offsets, self.arrays))


class Scatter:
    def __init__(self, links, columns, index, order):
        self.links = links
        self.index = index
        self.bits = bits_of(links.sizes["wide"])
        self.left = list(order[::-1])
        lead = (2,) * len(self.bits)
        size = links.sizes["wide"]
        self.base = [c.reshape(lead + (c.shape[0] // size, c.shape[1])) for c in columns]
        self.got = None
        self.at = None
        self.mine = None

    @property
    def arrays(self):
        return [self.base] if self.got is None else [self.base, self.got]

    @arrays.setter
    def arrays(self, values):
        self.base = values[0]
        if self.got is not None:
            self.got = values[1]

    def value(self):
        def pick(c):
            return lax.dynamic_index_in_dim(c, self.mine, self.at, keepdims=False)

        if self.got is None:
            return jnp.concatenate(self.base, -1) if len(self.base) > 1 else self.base[0]
        kept = jnp.concatenate([pick(c) for c in self.base], -1)
        return (kept.astype(F32) + self.got.astype(F32)).astype(LOW)

    def next(self):
        if not self.left:
            return
        bit = self.left.pop(0)
        at = self.bits.index(bit)
        mine = jnp.where((self.index & bit) != 0, 1, 0).astype(I32)
        if self.got is not None:
            self.base = [self.value()]
        send = jnp.concatenate(
            [lax.dynamic_index_in_dim(c, 1 - mine, at, keepdims=False) for c in self.base], -1
        )
        self.bits.pop(at)
        self.at, self.mine = at, mine
        self.got = self.links.swap(send, "wide", bit)

    def finish(self):
        while self.left:
            self.next()
        return self.value()


def sync(movers, *values):
    held = lax.optimization_barrier(([m.arrays for m in movers], values))
    for mover, arrays in zip(movers, held[0]):
        mover.arrays = arrays
    return held[1]


def order_of(order):
    offsets = [0]
    for bit in order:
        offsets = offsets + [k ^ bit for k in offsets]
    return offsets


def pack(index, narrow, shards, layouts):
    def kernel(index_ref, *refs):
        ins, outs, sems = refs[: len(shards)], refs[len(shards) : -1], refs[-1]
        at = index_ref[0]
        copies = []

        def add(source, target):
            copies.append(pltpu.make_async_copy(source, target, sems.at[len(copies)]))

        for (out, members), out_ref in zip(layouts, outs):
            low = 0
            for member, blocks, width in members:
                source = ins[member]
                if blocks is None:
                    size = source.shape[0] // narrow
                    row = pl.multiple_of(at * size, size)
                    cols = source.shape[1]
                    add(source.at[pl.ds(row, size), :], out_ref.at[0, :, low : low + cols])
                    low += cols
                    continue
                for block in range(blocks):
                    start = pl.multiple_of((block * narrow + at) * width, width)
                    add(source.at[:, pl.ds(start, width)], out_ref.at[0, :, low : low + width])
                    low += width
        for copy in copies:
            copy.start()
        for copy in copies:
            copy.wait()

    count = sum(1 if m[1] is None else m[1] for _, members in layouts for m in members)
    return pl.pallas_call(
        kernel,
        out_shape=[jax.ShapeDtypeStruct((1,) + shape, LOW) for shape, _ in layouts],
        in_specs=[SMEM_SPEC] + [ANY_SPEC] * len(shards),
        out_specs=[VMEM_SPEC] * len(layouts),
        scratch_shapes=[pltpu.SemaphoreType.DMA((count,))],
    )(index.reshape(1), *shards)


def assemble(sources, index, widths):
    own = sources[0][0][0][1].shape[1]
    arrays = [array for parts, _ in sources for _, array in parts]
    rows = sum(len(ks) for ks, _ in sources[0][0]) * own
    count = sum(len(ks) * len(spans) for parts, spans in sources for ks, _ in parts)

    def kernel(index_ref, *refs):
        ins, outs, sems = refs[: len(arrays)], refs[len(arrays) : -1], refs[-1]
        copies = []
        at_ref = 0
        for parts, spans in sources:
            for ks, _ in parts:
                for j, k in enumerate(ks):
                    row = pl.multiple_of((index_ref[0] ^ k) * own, own)
                    for low, high, out, at in spans:
                        copies.append(
                            pltpu.make_async_copy(
                                ins[at_ref].at[j, :, low:high],
                                outs[out].at[pl.ds(row, own), at : at + high - low],
                                sems.at[len(copies)],
                            )
                        )
                at_ref += 1
        for copy in copies:
            copy.start()
        for copy in copies:
            copy.wait()

    return pl.pallas_call(
        kernel,
        out_shape=[jax.ShapeDtypeStruct((rows, width), LOW) for width in widths],
        in_specs=[SMEM_SPEC] + [ANY_SPEC] * len(arrays),
        out_specs=[VMEM_SPEC] * len(widths),
        scratch_shapes=[pltpu.SemaphoreType.DMA((count,))],
    )(index.reshape(1), *arrays)


def head_columns(ref, part, head, heads, width):
    start = (part * heads + head) * width
    return ref[:, start : start + width]


def head_prob(query, key, bias):
    scores = dot_back(query, key) + bias
    lifted = jnp.exp(scores - jnp.max(scores, -1, keepdims=True))
    return lifted / jnp.sum(lifted, -1, keepdims=True)


def write_part(part_refs, value):
    for i, ref in enumerate(part_refs):

        @pl.when(pl.program_id(0) == i)
        def _():
            ref[...] = value


def attend_kernel(
    heads, normed_ref, qkv_ref, proj_ref, bias_ref, combined_ref, out_ref, *part_refs
):
    width = out_ref.shape[1] // heads
    bias = bias_ref[0]
    combined_ref[...] = dot_rows(normed_ref[...], qkv_ref[...]).astype(LOW)
    outs = []
    for head in range(heads):
        query = head_columns(combined_ref, 0, head, heads, width) * LOW(width**-0.5)
        key = head_columns(combined_ref, 1, head, heads, width)
        val = head_columns(combined_ref, 2, head, heads, width)
        prob = head_prob(query, key, bias).astype(LOW)
        outs.append(dot_rows(prob, val).astype(LOW))
    attended = jnp.concatenate(outs, 1)
    out_ref[...] = attended
    write_part(part_refs, dot_rows(attended, proj_ref[...]).astype(LOW))


def attend_back_kernel(
    heads, grad_ref, qkv_ref, proj_ref, bias_ref, combined_ref, out_ref, *rest
):
    part_refs, low_ref = rest[:-1], rest[-1]
    width = low_ref.shape[1] // heads
    scale = width**-0.5
    bias = bias_ref[0]
    low_ref[...] = dot_back(grad_ref[...], proj_ref[...]).astype(LOW)
    outs = [[], [], []]
    for head in range(heads):
        query = head_columns(combined_ref, 0, head, heads, width) * LOW(scale)
        key = head_columns(combined_ref, 1, head, heads, width)
        val = head_columns(combined_ref, 2, head, heads, width)
        grad = head_columns(low_ref, 0, head, heads, width)
        prob = head_prob(query, key, bias)
        prob_grad = dot_back(grad, val)
        inner = jnp.sum(prob * prob_grad, -1, keepdims=True)
        score_grad = (prob * (prob_grad - inner)).astype(LOW)
        outs[0].append((dot_rows(score_grad, key) * scale).astype(LOW))
        outs[1].append(dot_cross(score_grad, query).astype(LOW))
        outs[2].append(dot_cross(prob.astype(LOW), grad).astype(LOW))
    combined_grad = jnp.concatenate(outs[0] + outs[1] + outs[2], 1)
    out_ref[...] = combined_grad
    write_part(part_refs, dot_back(combined_grad, qkv_ref[...]).astype(LOW))


def attend_call(heads, values, qkv, proj, bias, combined=None):
    groups, rows, _ = bias.shape
    width = values.shape[1]
    third = proj.shape[0]
    total = groups * rows

    def rows_spec(cols):
        return pl.BlockSpec((rows, cols), lambda i: (i, 0))

    def whole_spec(array):
        return pl.BlockSpec(array.shape, lambda i: (0, 0))

    bias_spec = pl.BlockSpec((1, rows, rows), lambda i: (i, 0, 0))
    in_specs = [rows_spec(width), whole_spec(qkv), whole_spec(proj), bias_spec]
    wide_out = jax.ShapeDtypeStruct((total, 3 * third), LOW)
    part_outs = [jax.ShapeDtypeStruct((rows, width), LOW)] * groups
    part_specs = [pl.BlockSpec((rows, width), lambda i: (0, 0))] * groups
    if combined is None:
        return pl.pallas_call(
            functools.partial(attend_kernel, heads),
            grid=(groups,),
            out_shape=[wide_out, jax.ShapeDtypeStruct((total, third), LOW)] + part_outs,
            in_specs=in_specs,
            out_specs=[rows_spec(3 * third), rows_spec(third)] + part_specs,
        )(values, qkv, proj, bias)
    return pl.pallas_call(
        functools.partial(attend_back_kernel, heads),
        grid=(groups,),
        out_shape=[wide_out] + part_outs,
        in_specs=in_specs + [rows_spec(3 * third)],
        out_specs=[rows_spec(3 * third)] + part_specs,
        scratch_shapes=[pltpu.VMEM((rows, third), LOW)],
    )(values, qkv, proj, bias, combined)


def tile_call(body, outs, tiled, whole):
    rows = tiled[0].shape[0]
    block = min(rows, 128)
    count = len(tiled) + len(whole)

    def kernel(*refs):
        results = body(*[ref[...] for ref in refs[:count]])
        for ref, result in zip(refs[count:], results):
            ref[...] = result

    def rows_spec(cols):
        return pl.BlockSpec((block, cols), lambda i: (i, 0))

    return pl.pallas_call(
        kernel,
        grid=(rows // block,),
        out_shape=[jax.ShapeDtypeStruct((rows, cols), dtype) for cols, dtype in outs],
        in_specs=[rows_spec(t.shape[1]) for t in tiled]
        + [pl.BlockSpec(t.shape, lambda i: (0, 0)) for t in whole],
        out_specs=[rows_spec(cols) for cols, _ in outs],
    )(*tiled, *whole)


def cross(lefts, rights):
    out = dot_cross(lefts[0], rights[0])
    for left, right in zip(lefts[1:], rights[1:]):
        out = out + dot_cross(left, right)
    return out.astype(LOW)


def place(entries, index, order, plans):
    count = len(entries)
    own = entries[0].shape[0]
    weights = [plan[3] for plan in plans if plan[3] is not None]

    def kernel(index_ref, *refs):
        parts, weight_refs = refs[:count], list(refs[count : count + len(weights)])
        outs = list(refs[count + len(weights) :])

        def write(j, part_ref, out_refs):
            for (first, pieces, chunk, _), out_ref in zip(plans, out_refs):
                if chunk is None:
                    rows = pl.ds(pl.multiple_of(j * own, own), own)
                    out_ref[rows, :] = part_ref[:, first : first + pieces].astype(F32)
                    continue
                for p in range(pieces if chunk % 128 == 0 else 0):
                    at = pl.ds(pl.multiple_of((p * count + j) * chunk, chunk), chunk)
                    low = first + p * chunk
                    out_ref[:, at] = part_ref[:, low : low + chunk].astype(F32)

        def narrow_chunks(index, parts, out_ref, first, pieces, chunk):
            for j in range(count):
                for p in range(pieces):
                    low = first + p * chunk
                    value = parts[0][:, low : low + chunk].astype(F32)
                    for k, part_ref in zip(order[1:], parts[1:]):
                        other = part_ref[:, low : low + chunk].astype(F32)
                        value = jnp.where((index ^ j) == k, other, value)
                    at = (p * count + j) * chunk
                    out_ref[:, at : at + chunk] = value

        out_refs, sum_refs = [], []
        for plan in plans:
            out_refs.append(outs.pop(0))
            sum_refs.append(outs.pop(0) if plan[3] is not None else None)
        for k, part_ref in zip(order, parts):
            write(index_ref[0] ^ k, part_ref, out_refs)
        for (first, pieces, chunk, _), out_ref in zip(plans, out_refs):
            if chunk is not None and chunk % 128:
                narrow_chunks(index_ref[0], parts, out_ref, first, pieces, chunk)
        for out_ref, sum_ref in zip(out_refs, sum_refs):
            if sum_ref is not None:
                weight = weight_refs.pop(0)[...].astype(F32)
                sum_ref[...] = jnp.sum(weight * out_ref[...], -1, keepdims=True)

    shapes = []
    for _, pieces, chunk, weight in plans:
        if chunk is None:
            shapes.append((count * own, pieces))
        else:
            shapes.append((own, pieces * count * chunk))
        if weight is not None:
            shapes.append((own, 1))
    return pl.pallas_call(
        kernel,
        out_shape=[jax.ShapeDtypeStruct(shape, F32) for shape in shapes],
        in_specs=[SMEM_SPEC] + [VMEM_SPEC] * (count + len(weights)),
        out_specs=[VMEM_SPEC] * len(shapes),
    )(index.reshape(1), *entries, *weights)


def norm_stats(values):
    return lax.rsqrt(jnp.mean(values * values, -1, keepdims=True) + EPS)


def norm_back(values, scale, gain, grad):
    weighted = grad * gain
    inner = jnp.mean(weighted * values, -1, keepdims=True)
    return scale * (weighted - values * (scale * scale) * inner)


def gelu_parts(v):
    root = 0.7978845608028654
    inner = jnp.tanh(root * (v + 0.044715 * v * v * v))
    value = 0.5 * v * (1.0 + inner)
    slope = 0.5 * (1.0 + inner) + 0.5 * v * (1.0 - inner * inner) * root * (
        1.0 + 3.0 * 0.044715 * v * v
    )
    return value, slope


def make_device(wide, narrow):
    wide_bits = bits_of(wide)
    narrow_bits = bits_of(narrow)
    order_a = list(wide_bits)
    order_c = wide_bits[-1:] + wide_bits[:-1]
    near_order = order_of(narrow_bits)

    def per_device(
        tokens,
        segment_ids,
        routed_index,
        out_grad,
        dense_attn_gain,
        dense_qkv,
        dense_proj,
        dense_mlp_gain,
        dense_up,
        dense_down,
        routed_attn_gain,
        routed_qkv,
        routed_proj,
        routed_mlp_gain,
        routed_up,
        routed_down,
        router_vector,
    ):
        links = Links({"wide": wide, "narrow": narrow})
        w = lax.axis_index("wide").astype(I32)
        n = lax.axis_index("narrow").astype(I32)
        inputs = tokens[0].astype(F32)
        rows, width = inputs.shape
        segments = segment_ids[0]
        chosen = routed_index[0]
        cap = chosen.shape[0]
        heads = HEADS // narrow
        own = width // wide
        ffn = dense_up.shape[1]
        part = width // narrow
        unit = ffn // (wide * narrow)

        def pack_some(shards, kinds):
            def up_of(member):
                shard = shards[member].reshape(own, wide, narrow, unit)
                piece = lax.dynamic_index_in_dim(shard, n, 2, keepdims=False)
                return piece.reshape(own, ffn // narrow)

            def down_of(member):
                shard = shards[member].reshape(narrow, unit, width)
                return lax.dynamic_index_in_dim(shard, n, 0, keepdims=False)

            def attn_of(member):
                mixed = jnp.concatenate([shards[member], shards[member + 1]], 1)
                mixed = mixed.reshape(own, 4, narrow, part)
                piece = lax.dynamic_index_in_dim(mixed, n, 2, keepdims=False)
                return piece.reshape(own, 4 * part)

            layouts, pieces, member = [], [], 0
            for kind in kinds:
                if kind == "a":
                    members = [(member, 3, part), (member + 1, 1, part)]
                    layouts.append(((own, 4 * part), members))
                    pieces.append(lambda m=member: attn_of(m))
                elif kind == "u":
                    layouts.append(((own, ffn // narrow), [(member, wide, unit)]))
                    pieces.append(lambda m=member: up_of(m))
                else:
                    layouts.append(((unit, width), [(member, None, None)]))
                    pieces.append(lambda m=member: down_of(m))
                member += 2 if kind == "a" else 1
            if unit % 128 == 0:
                return pack(n, narrow, shards, layouts)
            return [piece()[None] for piece in pieces]

        def swap_blocks(array, axis):
            got = []
            for k in range(narrow):
                block = lax.dynamic_slice_in_dim(array, (n ^ k) * part, part, axis)
                got.append(block if k == 0 else links.swap(block, "narrow", k))
            return got

        def open_proj(proj_cols):
            return xor_blocks(jnp.concatenate(swap_blocks(proj_cols, 0), 1), n, narrow, 1)

        def open_rows(parts, columns):
            return assemble([(parts, [(0, columns, 0, 0)])], w, (columns,))[0]

        def proj_columns(proj_grad):
            return xor_blocks(jnp.concatenate(swap_blocks(proj_grad, 1), 0), n, narrow, 0)

        def flat(array):
            return array.reshape(-1, array.shape[-1])

        def share_core(local):
            return jnp.concatenate([local, links.swap(local, "narrow", 1)], 0)

        def swap_far(local):
            return links.swap(local, "narrow", 2)

        def share(local):
            got = [local] + [links.swap(local, "narrow", k) for k in range(1, narrow)]
            return jnp.stack(got, 0)

        def total(whole):
            parts = whole.reshape(narrow, -1, width)
            out = parts[0].astype(F32)
            for k in range(1, narrow):
                out = out + links.swap(parts[k], "narrow", k).astype(F32)
            return out

        def total_core(keep, send):
            return keep.astype(F32) + links.swap(send, "narrow", 1).astype(F32)

        def total_far(keep, send):
            return swap_far(total_core(keep, send).astype(LOW))

        def halves(chunk):
            half = chunk.shape[0] // 2
            return chunk[:half], chunk[half:]

        def normed_of(values, scale, gain):
            return (values * scale * gain).astype(LOW)

        def up_body(normed, up):
            pre = dot_rows(normed, up)
            return pre, gelu_parts(pre)[0].astype(LOW)

        def both_body(normed, grad, up, down):
            pre = dot_rows(normed, up)
            value, slope = gelu_parts(pre)
            active = value.astype(LOW)
            pre_grad = (slope * dot_back(grad, down)).astype(LOW)
            part = dot_back(pre_grad, up).astype(LOW)
            return active, dot_rows(active, down).astype(LOW), pre_grad, part

        def gain_grad(sums, gain):
            return sums[:, 0] / gain.astype(F32)

        def around(shard, far):
            others = [links.swap(part, "narrow", 1) for part in (shard, far)]
            return [shard, far] + others

        unit_all = ffn // narrow

        (piece_a,) = pack_some([dense_qkv, dense_proj], "a")
        split = 2 * part
        get_a = Gather(links, piece_a[:, :, :split], order_a)
        get_b = Gather(links, piece_a[:, :, split:], order_c)
        get_a.next()
        get_b.next()
        gains = jnp.stack([dense_attn_gain, dense_mlp_gain, routed_attn_gain, routed_mlp_gain])
        gains = links.gather(gains[None], "wide", order_a[:1])
        (gains,) = sync([get_a, get_b], gains)

        get_a.next(2)
        get_b.next()
        gains = links.gather(gains, "wide", order_a[1:])
        marks = share(jnp.concatenate([segments, chosen, jnp.take(segments, chosen)]))
        scale_0 = norm_stats(inputs)
        piece_u, piece_d, *pieces_r = pack_some(
            [dense_up, dense_down, routed_qkv, routed_proj, routed_up, routed_down], "udaud"
        )
        get_u = Gather(links, piece_u, order_a)
        get_d = Gather(links, piece_d, order_a)
        everything = [get_a, get_b, get_u, get_d]
        gains, scale_0, marks = sync(everything, gains, scale_0, marks)

        get_a.next()
        get_b.next(2)
        get_u.next()
        spread = order_of(order_a)
        places = jnp.array([spread.index(k) for k in range(wide)], I32)
        gains = jnp.take(gains, places[w ^ jnp.arange(wide, dtype=I32)], axis=0)
        gains = gains.transpose(1, 0, 2).reshape(4, width).astype(F32)
        normed = normed_of(inputs, scale_0, gains[0])
        far = swap_far(normed)
        normed_0 = [share_core(normed)]
        seg_all = marks[:, :rows]
        pos_r = marks[:, rows : rows + cap]
        seg_r = marks[:, rows + cap :].reshape(-1)
        where_r, of_r = pos_r.reshape(-1), jnp.repeat(jnp.arange(narrow, dtype=I32), cap)
        pos = jnp.arange(rows, dtype=I32)
        allowed = (pos[None, None, :] <= pos[None, :, None]) & (
            seg_all[:, None, :] == seg_all[:, :, None]
        )
        bias_0 = jnp.where(allowed, 0.0, NEG).astype(F32)
        bias_0 = [bias_0[: narrow // 2], bias_0[narrow // 2 :]]
        allowed = (where_r[None, :] <= where_r[:, None]) & (seg_r[None, :] == seg_r[:, None])
        allowed = allowed & (of_r[None, :] == of_r[:, None])
        bias_r = jnp.where(allowed, 0.0, NEG).astype(F32)[None]
        hits_all = (pos[None, :, None] == pos_r[:, None, :]).astype(LOW)
        gains, far, normed_0, bias_0, bias_r, hits_all, pieces_r = sync(
            everything, gains, far, normed_0, bias_0, bias_r, hits_all, pieces_r
        )
        full_ra, up_r, down_r = [
            lax.all_gather(piece[0], "wide", axis=0, tiled=True) for piece in pieces_r
        ]

        get_u.next(2)
        get_d.next()
        normed_0.append(share_core(far))
        qkv_d, proj_d = assemble(
            [
                (get_a.finish(), [(0, split, 0, 0)]),
                (get_b.finish(), [(0, part, 0, split), (part, 2 * part, 1, 0)]),
            ],
            w,
            (3 * part, part),
        )
        proj_d = open_proj(proj_d)
        second = attend_call(heads, normed_0[1], qkv_d, proj_d, bias_0[1])
        everything = [get_u, get_d]
        second, qkv_d, proj_d = sync(everything, second, qkv_d, proj_d)

        get_u.next()
        get_d.next()
        far = total_far(*second[2:])
        first = attend_call(heads, normed_0[0], qkv_d, proj_d, bias_0[0])
        combined_0 = [first[0], second[0]]
        attended_0 = [first[1], second[1]]
        near = total_core(*first[2:])
        near, far = sync(everything, near, far)

        get_d.next()
        hidden = inputs + near + far.astype(F32)
        scale_1 = norm_stats(hidden)
        normed = normed_of(hidden, scale_1, gains[1])
        far = swap_far(normed)
        normed_1 = [share_core(normed)]
        up_d = open_rows(get_u.finish(), unit_all)
        everything = everything[1:]
        first = tile_call(up_body, [(unit_all, F32), (unit_all, LOW)], normed_1, [up_d])
        first, far, up_d, hidden, scale_1 = sync(everything, first, far, up_d, hidden, scale_1)

        get_d.next()
        normed_1.append(share_core(far))
        second = tile_call(up_body, [(unit_all, F32), (unit_all, LOW)], [normed_1[1]], [up_d])
        pre_1 = [first[0], second[0]]
        active_1 = [first[1], second[1]]
        active_1, pre_1 = sync(everything, active_1, pre_1)

        down_d = open_rows(get_d.finish(), width)
        far = total_far(*[dot_rows(a, down_d).astype(LOW) for a in halves(active_1[1])])
        near = total_core(*[dot_rows(a, down_d).astype(LOW) for a in halves(active_1[0])])
        near, far, down_d = sync([], near, far, down_d)

        middle = hidden + near + far.astype(F32)
        selected = jnp.take(middle, chosen, axis=0)
        route_vec = router_vector.astype(F32)
        rate = jax.nn.sigmoid(jnp.dot(selected, route_vec, precision=HIGH))
        result_grad = out_grad[0]
        picked_grad = jnp.take(result_grad, chosen, axis=0).astype(F32)
        change_grad = rate[:, None] * picked_grad
        scale_2 = norm_stats(selected)
        normed_2 = flat(share(normed_of(selected, scale_2, gains[2])))
        qkv_r, proj_r = full_ra[:, : 3 * part], open_proj(full_ra[:, 3 * part :])
        combined_2, attended_2, part_2 = attend_call(heads, normed_2, qkv_r, proj_r, bias_r)
        routed_att = total(part_2)
        grad_3 = flat(share(change_grad.astype(LOW)))
        after = selected + routed_att
        scale_3 = norm_stats(after)
        normed_3 = flat(share(normed_of(after, scale_3, gains[3])))
        grad_1 = [share_core(result_grad), share_core(swap_far(result_grad))]

        active_3, routed_out, pre_grad_3, normed_part = tile_call(
            both_body,
            [(unit_all, LOW), (width, LOW), (unit_all, LOW), (width, LOW)],
            [normed_3, grad_3],
            [up_r, down_r],
        )
        both_r = jnp.concatenate(
            [cross([normed_3], [pre_grad_3]), cross([active_3], [grad_3])], 1
        )
        both_r, normed_part, routed_out, grad_1 = sync(
            [], both_r, normed_part, routed_out, grad_1
        )
        shard_r = lax.psum_scatter(both_r, "wide", scatter_dimension=0, tiled=True)

        after_grad = norm_back(after, scale_3, gains[3], total(normed_part))
        grad_2 = flat(share((change_grad + after_grad).astype(LOW)))
        proj_grad = proj_columns(cross([attended_2], [grad_2]))
        combined_grad_2, part_2 = attend_call(heads, grad_2, qkv_r, proj_r, bias_r, combined_2)
        change = routed_att + total(routed_out)
        put_ra = Scatter(links, [cross([normed_2], [combined_grad_2]), proj_grad], w, order_a)
        part_2, change = sync([put_ra], part_2, change)

        put_ra.next()
        rate_grad = jnp.sum(picked_grad * change, -1)
        logit_grad = rate_grad * rate * (1.0 - rate)
        att_in_grad = norm_back(selected, scale_2, gains[2], total(part_2))
        selected_grad = after_grad + att_in_grad + logit_grad[:, None] * route_vec[None, :]
        fresh = share((picked_grad + selected_grad).astype(LOW))
        router_total = jnp.dot(logit_grad, selected, precision=HIGH)
        hops = [("wide", bit) for bit in wide_bits[:-1]]
        hops += [("narrow", bit) for bit in narrow_bits[::-1]] + [("wide", wide_bits[-1])]

        def hop(value):
            if hops:
                value = value + links.swap(value, *hops.pop(0))
            return value

        router_total = hop(router_total)
        placed = jnp.einsum("sqk,skd->sqd", hits_all, fresh, preferred_element_type=F32)
        taken = jnp.any(hits_all != 0, -1, keepdims=True)
        half = narrow // 2
        grad_1 = [
            flat(jnp.where(taken[i * half : (i + 1) * half],
                           placed[i * half : (i + 1) * half].astype(LOW),
                           base.reshape(half, rows, width)))
            for i, base in enumerate(grad_1)
        ]
        put_d = Scatter(links, [cross(active_1, grad_1)], w, order_a)
        grad_1, selected_grad, router_total = sync([put_d], grad_1, selected_grad, router_total)

        put_d.next()

        def back_ffn(i):
            grad = dot_back(grad_1[i], down_d)
            pre_grad = (gelu_parts(pre_1[i])[1] * grad).astype(LOW)
            return pre_grad, dot_back(pre_grad, up_d).astype(LOW)

        second = back_ffn(1)
        far = total_far(*halves(second[1]))
        first = back_ffn(0)
        near = total_core(*halves(first[1]))
        pre_grad_1 = [first[0], second[0]]
        put_u = Scatter(links, [cross(normed_1, pre_grad_1)], w, order_a)
        router_total = hop(router_total)
        near, far, router_total = sync([put_u], near, far, router_total)

        put_u.next()
        hits = (pos[:, None] == chosen[None, :]).astype(F32)
        middle_grad = result_grad.astype(F32) + jnp.dot(hits, selected_grad, precision=HIGH)
        hidden_grad = middle_grad + norm_back(
            hidden, scale_1, gains[1], near + far.astype(F32)
        )
        hidden_low = hidden_grad.astype(LOW)
        far = swap_far(hidden_low)
        grad_0 = [share_core(hidden_low)]
        first = attend_call(heads, grad_0[0], qkv_d, proj_d, bias_0[0], combined_0[0])
        router_total = hop(router_total)
        moving = [put_ra, put_d]
        first, far, hidden_grad, router_total = sync(
            moving, first, far, hidden_grad, router_total
        )

        put_d.next()
        put_ra.next()
        grad_0.append(share_core(far))
        second = attend_call(heads, grad_0[1], qkv_d, proj_d, bias_0[1], combined_0[1])
        proj_grad = proj_columns(cross(attended_0, grad_0))
        combined_grad_0 = [first[0], second[0]]
        put_a = Scatter(links, [cross(normed_0, combined_grad_0), proj_grad], w, order_a)
        router_total = hop(router_total)
        moving = [put_ra, put_d, put_u, put_a]
        first, second, router_total = sync(moving, first[1:], second[1:], router_total)

        put_a.next()
        put_u.next()
        put_d.next()
        put_ra.next()
        far_rf = swap_far(shard_r)
        far = total_far(*second)
        near = total_core(*first)
        input_part = norm_back(inputs, scale_0, gains[0], near + far.astype(F32))
        input_total = (hidden_grad + input_part).astype(LOW)
        added = jnp.dot(hits, rate[:, None] * change, precision=HIGH)
        result = (middle + added).astype(LOW)
        moving = [put_ra, put_d, put_u, put_a]
        input_total, result, router_total, far_rf = sync(
            moving, input_total, result, router_total, far_rf
        )

        def plans_f(weight):
            return [(0, wide, unit, weight), (unit_all, width, None, None)]

        def plans_a(weight):
            return [(0, 3, part, weight), (3 * part, 1, part, None)]

        put_a.next()
        put_u.next()
        shard_ra, shard_d = put_ra.finish(), put_d.finish()
        far_ra, far_d = swap_far(shard_ra), swap_far(shard_d)
        out_up_r, gain_ru, out_down_r = place(
            around(shard_r, far_rf), n, near_order, plans_f(routed_up)
        )
        while hops:
            router_total = hop(router_total)
        far_ra, far_d, gain_ru, router_total = sync(
            [put_a, put_u], far_ra, far_d, gain_ru, router_total
        )

        put_a.next()
        shard_u = put_u.finish()
        far_u = swap_far(shard_u)
        out_qkv_r, gain_ra, out_proj_r = place(
            around(shard_ra, far_ra), n, near_order, plans_a(routed_qkv)
        )
        (out_down,) = place(around(shard_d, far_d), n, near_order, [(0, width, None, None)])
        far_u, gain_ra, out_down = sync([put_a], far_u, gain_ra, out_down)

        shard_a = put_a.finish()
        far_a = swap_far(shard_a)
        out_up, gain_u = place(
            around(shard_u, far_u), n, near_order, [(0, wide, unit, dense_up)]
        )
        out_qkv, gain_a, out_proj = place(
            around(shard_a, far_a), n, near_order, plans_a(dense_qkv)
        )
        return (
            result[None],
            input_total[None],
            gain_grad(gain_a, dense_attn_gain),
            out_qkv,
            out_proj,
            gain_grad(gain_u, dense_mlp_gain),
            out_up,
            out_down,
            gain_grad(gain_ra, routed_attn_gain),
            out_qkv_r,
            out_proj_r,
            gain_grad(gain_ru, routed_mlp_gain),
            out_up_r,
            out_down_r,
            router_total,
        )

    return per_device


def solution(mesh):
    both = P(("wide", "narrow"))
    wide = P("wide")
    weights = (wide,) * 6
    return jax.shard_map(
        make_device(mesh.shape["wide"], mesh.shape["narrow"]),
        mesh=mesh,
        in_specs=(both, both, both, both) + weights + weights + (P(),),
        out_specs=(both, both) + weights + weights + (P(),),
        check_vma=False,
    )
```

```python
import functools

import jax
import jax.numpy as jnp
from jax import lax
from jax.experimental import pallas as pl
from jax.experimental.pallas import tpu as pltpu
from jax.sharding import PartitionSpec as P

HEADS = 16
EPS = 1e-06
NEG = -1e30
HIGH = lax.Precision.HIGHEST
LOW = jnp.bfloat16
F32 = jnp.float32
I32 = jnp.int32
VMEM_SPEC = pl.BlockSpec(memory_space=pltpu.VMEM)
SMEM_SPEC = pl.BlockSpec(memory_space=pltpu.SMEM)
ANY_SPEC = pl.BlockSpec(memory_space=pl.ANY)


def dot_rows(left, right):
    return jnp.dot(left, right, preferred_element_type=F32)


def dot_cross(left, right):
    return lax.dot_general(left, right, (((0,), (0,)), ((), ())), preferred_element_type=F32)


def dot_back(left, right):
    return lax.dot_general(left, right, (((1,), (1,)), ((), ())), preferred_element_type=F32)


def bits_of(size):
    found = []
    bit = size // 2
    while bit >= 1:
        found.append(bit)
        bit //= 2
    return found


def xor_blocks(array, index, blocks, axis):
    size = array.shape[axis] // blocks
    for bit in bits_of(blocks):
        parts = [
            lax.slice_in_dim(array, k * size, (k + 1) * size, axis=axis) for k in range(blocks)
        ]
        swapped = jnp.concatenate([parts[k ^ bit] for k in range(blocks)], axis=axis)
        array = jnp.where((index & bit) != 0, swapped, array)
    return array


class Links:
    def __init__(self, sizes):
        self.sizes = sizes

    def swap(self, array, axis, bit):
        return lax.ppermute(array, axis, [(i, i ^ bit) for i in range(self.sizes[axis])])

    def gather(self, local, axis, order):
        for bit in order:
            local = jnp.concatenate([local, self.swap(local, axis, bit)], 0)
        return local


class Gather:
    def __init__(self, links, piece, order):
        self.links = links
        self.arrays = [piece]
        self.offsets = [[0]]
        self.todo = [(order[0], None)]
        made = 1
        for bit in order[1:]:
            self.todo += [(bit, i) for i in range(made)]
            made *= 2

    def next(self, count=1):
        for bit, at in self.todo[:count]:
            got = self.links.swap(self.arrays[at or 0], "wide", bit)
            offsets = [k ^ bit for k in self.offsets[at or 0]]
            if at is None:
                self.arrays = [jnp.concatenate([self.arrays[0], got], 0)]
                self.offsets = [self.offsets[0] + offsets]
            else:
                self.arrays.append(got)
                self.offsets.append(offsets)
        self.todo = self.todo[count:]

    def finish(self):
        self.next(len(self.todo))
        return list(zip(self.offsets, self.arrays))


class Scatter:
    def __init__(self, links, columns, index, order):
        self.links = links
        self.index = index
        self.bits = bits_of(links.sizes["wide"])
        self.left = list(order[::-1])
        lead = (2,) * len(self.bits)
        size = links.sizes["wide"]
        self.base = [c.reshape(lead + (c.shape[0] // size, c.shape[1])) for c in columns]
        self.got = None
        self.at = None
        self.mine = None

    @property
    def arrays(self):
        return [self.base] if self.got is None else [self.base, self.got]

    @arrays.setter
    def arrays(self, values):
        self.base = values[0]
        if self.got is not None:
            self.got = values[1]

    def value(self):
        def pick(c):
            return lax.dynamic_index_in_dim(c, self.mine, self.at, keepdims=False)

        if self.got is None:
            return jnp.concatenate(self.base, -1) if len(self.base) > 1 else self.base[0]
        kept = jnp.concatenate([pick(c) for c in self.base], -1)
        return (kept.astype(F32) + self.got.astype(F32)).astype(LOW)

    def next(self):
        if not self.left:
            return
        bit = self.left.pop(0)
        at = self.bits.index(bit)
        mine = jnp.where((self.index & bit) != 0, 1, 0).astype(I32)
        if self.got is not None:
            self.base = [self.value()]
        send = jnp.concatenate(
            [lax.dynamic_index_in_dim(c, 1 - mine, at, keepdims=False) for c in self.base], -1
        )
        self.bits.pop(at)
        self.at, self.mine = at, mine
        self.got = self.links.swap(send, "wide", bit)

    def finish(self):
        while self.left:
            self.next()
        return self.value()


def sync(movers, *values):
    held = lax.optimization_barrier(([m.arrays for m in movers], values))
    for mover, arrays in zip(movers, held[0]):
        mover.arrays = arrays
    return held[1]


def order_of(order):
    offsets = [0]
    for bit in order:
        offsets = offsets + [k ^ bit for k in offsets]
    return offsets


def pack(index, narrow, shards, layouts):
    def kernel(index_ref, *refs):
        ins, outs, sems = refs[: len(shards)], refs[len(shards) : -1], refs[-1]
        at = index_ref[0]
        copies = []

        def add(source, target):
            copies.append(pltpu.make_async_copy(source, target, sems.at[len(copies)]))

        for (out, members), out_ref in zip(layouts, outs):
            low = 0
            for member, blocks, width in members:
                source = ins[member]
                if blocks is None:
                    size = source.shape[0] // narrow
                    row = pl.multiple_of(at * size, size)
                    cols = source.shape[1]
                    add(source.at[pl.ds(row, size), :], out_ref.at[0, :, low : low + cols])
                    low += cols
                    continue
                for block in range(blocks):
                    start = pl.multiple_of((block * narrow + at) * width, width)
                    add(source.at[:, pl.ds(start, width)], out_ref.at[0, :, low : low + width])
                    low += width
        for copy in copies:
            copy.start()
        for copy in copies:
            copy.wait()

    count = sum(1 if m[1] is None else m[1] for _, members in layouts for m in members)
    return pl.pallas_call(
        kernel,
        out_shape=[jax.ShapeDtypeStruct((1,) + shape, LOW) for shape, _ in layouts],
        in_specs=[SMEM_SPEC] + [ANY_SPEC] * len(shards),
        out_specs=[VMEM_SPEC] * len(layouts),
        scratch_shapes=[pltpu.SemaphoreType.DMA((count,))],
    )(index.reshape(1), *shards)


def assemble(sources, index, widths):
    own = sources[0][0][0][1].shape[1]
    arrays = [array for parts, _ in sources for _, array in parts]
    rows = sum(len(ks) for ks, _ in sources[0][0]) * own
    count = sum(len(ks) * len(spans) for parts, spans in sources for ks, _ in parts)

    def kernel(index_ref, *refs):
        ins, outs, sems = refs[: len(arrays)], refs[len(arrays) : -1], refs[-1]
        copies = []
        at_ref = 0
        for parts, spans in sources:
            for ks, _ in parts:
                for j, k in enumerate(ks):
                    row = pl.multiple_of((index_ref[0] ^ k) * own, own)
                    for low, high, out, at in spans:
                        copies.append(
                            pltpu.make_async_copy(
                                ins[at_ref].at[j, :, low:high],
                                outs[out].at[pl.ds(row, own), at : at + high - low],
                                sems.at[len(copies)],
                            )
                        )
                at_ref += 1
        for copy in copies:
            copy.start()
        for copy in copies:
            copy.wait()

    return pl.pallas_call(
        kernel,
        out_shape=[jax.ShapeDtypeStruct((rows, width), LOW) for width in widths],
        in_specs=[SMEM_SPEC] + [ANY_SPEC] * len(arrays),
        out_specs=[VMEM_SPEC] * len(widths),
        scratch_shapes=[pltpu.SemaphoreType.DMA((count,))],
    )(index.reshape(1), *arrays)


def head_columns(ref, part, head, heads, width):
    start = (part * heads + head) * width
    return ref[:, start : start + width]


def head_prob(query, key, bias):
    scores = dot_back(query, key) + bias
    lifted = jnp.exp(scores - jnp.max(scores, -1, keepdims=True))
    return lifted / jnp.sum(lifted, -1, keepdims=True)


def write_part(part_refs, value):
    for i, ref in enumerate(part_refs):

        @pl.when(pl.program_id(0) == i)
        def _():
            ref[...] = value


def attend_kernel(
    heads, normed_ref, qkv_ref, proj_ref, bias_ref, combined_ref, out_ref, *part_refs
):
    width = out_ref.shape[1] // heads
    bias = bias_ref[0]
    combined_ref[...] = dot_rows(normed_ref[...], qkv_ref[...]).astype(LOW)
    outs = []
    for head in range(heads):
        query = head_columns(combined_ref, 0, head, heads, width) * LOW(width**-0.5)
        key = head_columns(combined_ref, 1, head, heads, width)
        val = head_columns(combined_ref, 2, head, heads, width)
        prob = head_prob(query, key, bias).astype(LOW)
        outs.append(dot_rows(prob, val).astype(LOW))
    attended = jnp.concatenate(outs, 1)
    out_ref[...] = attended
    write_part(part_refs, dot_rows(attended, proj_ref[...]).astype(LOW))


def attend_back_kernel(
    heads, grad_ref, qkv_ref, proj_ref, bias_ref, combined_ref, out_ref, *rest
):
    part_refs, low_ref = rest[:-1], rest[-1]
    width = low_ref.shape[1] // heads
    scale = width**-0.5
    bias = bias_ref[0]
    low_ref[...] = dot_back(grad_ref[...], proj_ref[...]).astype(LOW)
    outs = [[], [], []]
    for head in range(heads):
        query = head_columns(combined_ref, 0, head, heads, width) * LOW(scale)
        key = head_columns(combined_ref, 1, head, heads, width)
        val = head_columns(combined_ref, 2, head, heads, width)
        grad = head_columns(low_ref, 0, head, heads, width)
        prob = head_prob(query, key, bias)
        prob_grad = dot_back(grad, val)
        inner = jnp.sum(prob * prob_grad, -1, keepdims=True)
        score_grad = (prob * (prob_grad - inner)).astype(LOW)
        outs[0].append((dot_rows(score_grad, key) * scale).astype(LOW))
        outs[1].append(dot_cross(score_grad, query).astype(LOW))
        outs[2].append(dot_cross(prob.astype(LOW), grad).astype(LOW))
    combined_grad = jnp.concatenate(outs[0] + outs[1] + outs[2], 1)
    out_ref[...] = combined_grad
    write_part(part_refs, dot_back(combined_grad, qkv_ref[...]).astype(LOW))


def attend_call(heads, values, qkv, proj, bias, combined=None):
    groups, rows, _ = bias.shape
    width = values.shape[1]
    third = proj.shape[0]
    total = groups * rows

    def rows_spec(cols):
        return pl.BlockSpec((rows, cols), lambda i: (i, 0))

    def whole_spec(array):
        return pl.BlockSpec(array.shape, lambda i: (0, 0))

    bias_spec = pl.BlockSpec((1, rows, rows), lambda i: (i, 0, 0))
    in_specs = [rows_spec(width), whole_spec(qkv), whole_spec(proj), bias_spec]
    wide_out = jax.ShapeDtypeStruct((total, 3 * third), LOW)
    part_outs = [jax.ShapeDtypeStruct((rows, width), LOW)] * groups
    part_specs = [pl.BlockSpec((rows, width), lambda i: (0, 0))] * groups
    if combined is None:
        return pl.pallas_call(
            functools.partial(attend_kernel, heads),
            grid=(groups,),
            out_shape=[wide_out, jax.ShapeDtypeStruct((total, third), LOW)] + part_outs,
            in_specs=in_specs,
            out_specs=[rows_spec(3 * third), rows_spec(third)] + part_specs,
        )(values, qkv, proj, bias)
    return pl.pallas_call(
        functools.partial(attend_back_kernel, heads),
        grid=(groups,),
        out_shape=[wide_out] + part_outs,
        in_specs=in_specs + [rows_spec(3 * third)],
        out_specs=[rows_spec(3 * third)] + part_specs,
        scratch_shapes=[pltpu.VMEM((rows, third), LOW)],
    )(values, qkv, proj, bias, combined)


def tile_call(body, outs, tiled, whole):
    rows = tiled[0].shape[0]
    block = min(rows, 128)
    count = len(tiled) + len(whole)

    def kernel(*refs):
        results = body(*[ref[...] for ref in refs[:count]])
        for ref, result in zip(refs[count:], results):
            ref[...] = result

    def rows_spec(cols):
        return pl.BlockSpec((block, cols), lambda i: (i, 0))

    return pl.pallas_call(
        kernel,
        grid=(rows // block,),
        out_shape=[jax.ShapeDtypeStruct((rows, cols), dtype) for cols, dtype in outs],
        in_specs=[rows_spec(t.shape[1]) for t in tiled]
        + [pl.BlockSpec(t.shape, lambda i: (0, 0)) for t in whole],
        out_specs=[rows_spec(cols) for cols, _ in outs],
    )(*tiled, *whole)


def cross(lefts, rights):
    out = dot_cross(lefts[0], rights[0])
    for left, right in zip(lefts[1:], rights[1:]):
        out = out + dot_cross(left, right)
    return out.astype(LOW)


def place(entries, index, order, plans):
    count = len(entries)
    own = entries[0].shape[0]
    weights = [plan[3] for plan in plans if plan[3] is not None]

    def kernel(index_ref, *refs):
        parts, weight_refs = refs[:count], list(refs[count : count + len(weights)])
        outs = list(refs[count + len(weights) :])

        def write(j, part_ref, out_refs):
            for (first, pieces, chunk, _), out_ref in zip(plans, out_refs):
                if chunk is None:
                    rows = pl.ds(pl.multiple_of(j * own, own), own)
                    out_ref[rows, :] = part_ref[:, first : first + pieces].astype(F32)
                    continue
                for p in range(pieces if chunk % 128 == 0 else 0):
                    at = pl.ds(pl.multiple_of((p * count + j) * chunk, chunk), chunk)
                    low = first + p * chunk
                    out_ref[:, at] = part_ref[:, low : low + chunk].astype(F32)

        def narrow_chunks(index, parts, out_ref, first, pieces, chunk):
            for j in range(count):
                for p in range(pieces):
                    low = first + p * chunk
                    value = parts[0][:, low : low + chunk].astype(F32)
                    for k, part_ref in zip(order[1:], parts[1:]):
                        other = part_ref[:, low : low + chunk].astype(F32)
                        value = jnp.where((index ^ j) == k, other, value)
                    at = (p * count + j) * chunk
                    out_ref[:, at : at + chunk] = value

        out_refs, sum_refs = [], []
        for plan in plans:
            out_refs.append(outs.pop(0))
            sum_refs.append(outs.pop(0) if plan[3] is not None else None)
        for k, part_ref in zip(order, parts):
            write(index_ref[0] ^ k, part_ref, out_refs)
        for (first, pieces, chunk, _), out_ref in zip(plans, out_refs):
            if chunk is not None and chunk % 128:
                narrow_chunks(index_ref[0], parts, out_ref, first, pieces, chunk)
        for out_ref, sum_ref in zip(out_refs, sum_refs):
            if sum_ref is not None:
                weight = weight_refs.pop(0)[...].astype(F32)
                sum_ref[...] = jnp.sum(weight * out_ref[...], -1, keepdims=True)

    shapes = []
    for _, pieces, chunk, weight in plans:
        if chunk is None:
            shapes.append((count * own, pieces))
        else:
            shapes.append((own, pieces * count * chunk))
        if weight is not None:
            shapes.append((own, 1))
    return pl.pallas_call(
        kernel,
        out_shape=[jax.ShapeDtypeStruct(shape, F32) for shape in shapes],
        in_specs=[SMEM_SPEC] + [VMEM_SPEC] * (count + len(weights)),
        out_specs=[VMEM_SPEC] * len(shapes),
    )(index.reshape(1), *entries, *weights)


def norm_stats(values):
    return lax.rsqrt(jnp.mean(values * values, -1, keepdims=True) + EPS)


def norm_back(values, scale, gain, grad):
    weighted = grad * gain
    inner = jnp.mean(weighted * values, -1, keepdims=True)
    return scale * (weighted - values * (scale * scale) * inner)


def gelu_parts(v):
    root = 0.7978845608028654
    inner = jnp.tanh(root * (v + 0.044715 * v * v * v))
    value = 0.5 * v * (1.0 + inner)
    slope = 0.5 * (1.0 + inner) + 0.5 * v * (1.0 - inner * inner) * root * (
        1.0 + 3.0 * 0.044715 * v * v
    )
    return value, slope


def make_device(wide, narrow):
    wide_bits = bits_of(wide)
    narrow_bits = bits_of(narrow)
    order_a = list(wide_bits)
    order_c = wide_bits[-1:] + wide_bits[:-1]
    near_order = order_of(narrow_bits)

    def per_device(
        tokens,
        segment_ids,
        routed_index,
        out_grad,
        dense_attn_gain,
        dense_qkv,
        dense_proj,
        dense_mlp_gain,
        dense_up,
        dense_down,
        routed_attn_gain,
        routed_qkv,
        routed_proj,
        routed_mlp_gain,
        routed_up,
        routed_down,
        router_vector,
    ):
        links = Links({"wide": wide, "narrow": narrow})
        w = lax.axis_index("wide").astype(I32)
        n = lax.axis_index("narrow").astype(I32)
        inputs = tokens[0].astype(F32)
        rows, width = inputs.shape
        segments = segment_ids[0]
        chosen = routed_index[0]
        cap = chosen.shape[0]
        heads = HEADS // narrow
        own = width // wide
        ffn = dense_up.shape[1]
        part = width // narrow
        unit = ffn // (wide * narrow)

        def pack_some(shards, kinds):
            def up_of(member):
                shard = shards[member].reshape(own, wide, narrow, unit)
                piece = lax.dynamic_index_in_dim(shard, n, 2, keepdims=False)
                return piece.reshape(own, ffn // narrow)

            def down_of(member):
                shard = shards[member].reshape(narrow, unit, width)
                return lax.dynamic_index_in_dim(shard, n, 0, keepdims=False)

            def attn_of(member):
                mixed = jnp.concatenate([shards[member], shards[member + 1]], 1)
                mixed = mixed.reshape(own, 4, narrow, part)
                piece = lax.dynamic_index_in_dim(mixed, n, 2, keepdims=False)
                return piece.reshape(own, 4 * part)

            layouts, pieces, member = [], [], 0
            for kind in kinds:
                if kind == "a":
                    members = [(member, 3, part), (member + 1, 1, part)]
                    layouts.append(((own, 4 * part), members))
                    pieces.append(lambda m=member: attn_of(m))
                elif kind == "u":
                    layouts.append(((own, ffn // narrow), [(member, wide, unit)]))
                    pieces.append(lambda m=member: up_of(m))
                else:
                    layouts.append(((unit, width), [(member, None, None)]))
                    pieces.append(lambda m=member: down_of(m))
                member += 2 if kind == "a" else 1
            if unit % 128 == 0:
                return pack(n, narrow, shards, layouts)
            return [piece()[None] for piece in pieces]

        def swap_blocks(array, axis):
            got = []
            for k in range(narrow):
                block = lax.dynamic_slice_in_dim(array, (n ^ k) * part, part, axis)
                got.append(block if k == 0 else links.swap(block, "narrow", k))
            return got

        def open_proj(proj_cols):
            return xor_blocks(jnp.concatenate(swap_blocks(proj_cols, 0), 1), n, narrow, 1)

        def open_rows(parts, columns):
            return assemble([(parts, [(0, columns, 0, 0)])], w, (columns,))[0]

        def proj_columns(proj_grad):
            return xor_blocks(jnp.concatenate(swap_blocks(proj_grad, 1), 0), n, narrow, 0)

        def flat(array):
            return array.reshape(-1, array.shape[-1])

        def share_core(local):
            return jnp.concatenate([local, links.swap(local, "narrow", 1)], 0)

        def swap_far(local):
            return links.swap(local, "narrow", 2)

        def share(local):
            got = [local] + [links.swap(local, "narrow", k) for k in range(1, narrow)]
            return jnp.stack(got, 0)

        def total(whole):
            parts = whole.reshape(narrow, -1, width)
            out = parts[0].astype(F32)
            for k in range(1, narrow):
                out = out + links.swap(parts[k], "narrow", k).astype(F32)
            return out

        def total_core(keep, send):
            return keep.astype(F32) + links.swap(send, "narrow", 1).astype(F32)

        def total_far(keep, send):
            return swap_far(total_core(keep, send).astype(LOW))

        def halves(chunk):
            half = chunk.shape[0] // 2
            return chunk[:half], chunk[half:]

        def normed_of(values, scale, gain):
            return (values * scale * gain).astype(LOW)

        def up_body(normed, up):
            pre = dot_rows(normed, up)
            return pre, gelu_parts(pre)[0].astype(LOW)

        def both_body(normed, grad, up, down):
            pre = dot_rows(normed, up)
            value, slope = gelu_parts(pre)
            active = value.astype(LOW)
            pre_grad = (slope * dot_back(grad, down)).astype(LOW)
            part = dot_back(pre_grad, up).astype(LOW)
            return active, dot_rows(active, down).astype(LOW), pre_grad, part

        def gain_grad(sums, gain):
            return sums[:, 0] / gain.astype(F32)

        def around(shard, far):
            others = [links.swap(part, "narrow", 1) for part in (shard, far)]
            return [shard, far] + others

        unit_all = ffn // narrow

        (piece_a,) = pack_some([dense_qkv, dense_proj], "a")
        split = 2 * part
        get_a = Gather(links, piece_a[:, :, :split], order_a)
        get_b = Gather(links, piece_a[:, :, split:], order_c)
        get_a.next()
        get_b.next()
        gains = jnp.stack([dense_attn_gain, dense_mlp_gain, routed_attn_gain, routed_mlp_gain])
        gains = links.gather(gains[None], "wide", order_a[:1])
        (gains,) = sync([get_a, get_b], gains)

        get_a.next(2)
        get_b.next()
        gains = links.gather(gains, "wide", order_a[1:])
        marks = share(jnp.concatenate([segments, chosen, jnp.take(segments, chosen)]))
        scale_0 = norm_stats(inputs)
        piece_u, piece_d, *pieces_r = pack_some(
            [dense_up, dense_down, routed_qkv, routed_proj, routed_up, routed_down], "udaud"
        )
        get_u = Gather(links, piece_u, order_a)
        get_d = Gather(links, piece_d, order_a)
        everything = [get_a, get_b, get_u, get_d]
        gains, scale_0, marks = sync(everything, gains, scale_0, marks)

        get_a.next()
        get_b.next(2)
        get_u.next()
        spread = order_of(order_a)
        places = jnp.array([spread.index(k) for k in range(wide)], I32)
        gains = jnp.take(gains, places[w ^ jnp.arange(wide, dtype=I32)], axis=0)
        gains = gains.transpose(1, 0, 2).reshape(4, width).astype(F32)
        normed = normed_of(inputs, scale_0, gains[0])
        far = swap_far(normed)
        normed_0 = [share_core(normed)]
        seg_all = marks[:, :rows]
        pos_r = marks[:, rows : rows + cap]
        seg_r = marks[:, rows + cap :].reshape(-1)
        where_r, of_r = pos_r.reshape(-1), jnp.repeat(jnp.arange(narrow, dtype=I32), cap)
        pos = jnp.arange(rows, dtype=I32)
        allowed = (pos[None, None, :] <= pos[None, :, None]) & (
            seg_all[:, None, :] == seg_all[:, :, None]
        )
        bias_0 = jnp.where(allowed, 0.0, NEG).astype(F32)
        bias_0 = [bias_0[: narrow // 2], bias_0[narrow // 2 :]]
        allowed = (where_r[None, :] <= where_r[:, None]) & (seg_r[None, :] == seg_r[:, None])
        allowed = allowed & (of_r[None, :] == of_r[:, None])
        bias_r = jnp.where(allowed, 0.0, NEG).astype(F32)[None]
        hits_all = (pos[None, :, None] == pos_r[:, None, :]).astype(LOW)
        gains, far, normed_0, bias_0, bias_r, hits_all, pieces_r = sync(
            everything, gains, far, normed_0, bias_0, bias_r, hits_all, pieces_r
        )
        full_ra, up_r, down_r = [
            lax.all_gather(piece[0], "wide", axis=0, tiled=True) for piece in pieces_r
        ]

        get_u.next(2)
        get_d.next()
        normed_0.append(share_core(far))
        qkv_d, proj_d = assemble(
            [
                (get_a.finish(), [(0, split, 0, 0)]),
                (get_b.finish(), [(0, part, 0, split), (part, 2 * part, 1, 0)]),
            ],
            w,
            (3 * part, part),
        )
        proj_d = open_proj(proj_d)
        second = attend_call(heads, normed_0[1], qkv_d, proj_d, bias_0[1])
        everything = [get_u, get_d]
        second, qkv_d, proj_d = sync(everything, second, qkv_d, proj_d)

        get_u.next()
        get_d.next()
        far = total_far(*second[2:])
        first = attend_call(heads, normed_0[0], qkv_d, proj_d, bias_0[0])
        combined_0 = [first[0], second[0]]
        attended_0 = [first[1], second[1]]
        near = total_core(*first[2:])
        near, far = sync(everything, near, far)

        get_d.next()
        hidden = inputs + near + far.astype(F32)
        scale_1 = norm_stats(hidden)
        normed = normed_of(hidden, scale_1, gains[1])
        far = swap_far(normed)
        normed_1 = [share_core(normed)]
        up_d = open_rows(get_u.finish(), unit_all)
        everything = everything[1:]
        first = tile_call(up_body, [(unit_all, F32), (unit_all, LOW)], normed_1, [up_d])
        first, far, up_d, hidden, scale_1 = sync(everything, first, far, up_d, hidden, scale_1)

        get_d.next()
        normed_1.append(share_core(far))
        second = tile_call(up_body, [(unit_all, F32), (unit_all, LOW)], [normed_1[1]], [up_d])
        pre_1 = [first[0], second[0]]
        active_1 = [first[1], second[1]]
        active_1, pre_1 = sync(everything, active_1, pre_1)

        down_d = open_rows(get_d.finish(), width)
        far = total_far(*[dot_rows(a, down_d).astype(LOW) for a in halves(active_1[1])])
        near = total_core(*[dot_rows(a, down_d).astype(LOW) for a in halves(active_1[0])])
        near, far, down_d = sync([], near, far, down_d)

        middle = hidden + near + far.astype(F32)
        selected = jnp.take(middle, chosen, axis=0)
        route_vec = router_vector.astype(F32)
        rate = jax.nn.sigmoid(jnp.dot(selected, route_vec, precision=HIGH))
        result_grad = out_grad[0]
        picked_grad = jnp.take(result_grad, chosen, axis=0).astype(F32)
        change_grad = rate[:, None] * picked_grad
        scale_2 = norm_stats(selected)
        normed_2 = flat(share(normed_of(selected, scale_2, gains[2])))
        qkv_r, proj_r = full_ra[:, : 3 * part], open_proj(full_ra[:, 3 * part :])
        combined_2, attended_2, part_2 = attend_call(heads, normed_2, qkv_r, proj_r, bias_r)
        routed_att = total(part_2)
        grad_3 = flat(share(change_grad.astype(LOW)))
        after = selected + routed_att
        scale_3 = norm_stats(after)
        normed_3 = flat(share(normed_of(after, scale_3, gains[3])))
        grad_1 = [share_core(result_grad), share_core(swap_far(result_grad))]

        active_3, routed_out, pre_grad_3, normed_part = tile_call(
            both_body,
            [(unit_all, LOW), (width, LOW), (unit_all, LOW), (width, LOW)],
            [normed_3, grad_3],
            [up_r, down_r],
        )
        both_r = jnp.concatenate(
            [cross([normed_3], [pre_grad_3]), cross([active_3], [grad_3])], 1
        )
        both_r, normed_part, routed_out, grad_1 = sync(
            [], both_r, normed_part, routed_out, grad_1
        )
        shard_r = lax.psum_scatter(both_r, "wide", scatter_dimension=0, tiled=True)

        after_grad = norm_back(after, scale_3, gains[3], total(normed_part))
        grad_2 = flat(share((change_grad + after_grad).astype(LOW)))
        proj_grad = proj_columns(cross([attended_2], [grad_2]))
        combined_grad_2, part_2 = attend_call(heads, grad_2, qkv_r, proj_r, bias_r, combined_2)
        change = routed_att + total(routed_out)
        put_ra = Scatter(links, [cross([normed_2], [combined_grad_2]), proj_grad], w, order_c)
        part_2, change = sync([put_ra], part_2, change)

        put_ra.next()
        rate_grad = jnp.sum(picked_grad * change, -1)
        logit_grad = rate_grad * rate * (1.0 - rate)
        att_in_grad = norm_back(selected, scale_2, gains[2], total(part_2))
        selected_grad = after_grad + att_in_grad + logit_grad[:, None] * route_vec[None, :]
        fresh = share((picked_grad + selected_grad).astype(LOW))
        router_total = jnp.dot(logit_grad, selected, precision=HIGH)
        hops = [("wide", bit) for bit in wide_bits[:-1]]
        hops += [("narrow", bit) for bit in narrow_bits[::-1]] + [("wide", wide_bits[-1])]

        def hop(value):
            if hops:
                value = value + links.swap(value, *hops.pop(0))
            return value

        router_total = hop(router_total)
        placed = jnp.einsum("sqk,skd->sqd", hits_all, fresh, preferred_element_type=F32)
        taken = jnp.any(hits_all != 0, -1, keepdims=True)
        half = narrow // 2
        grad_1 = [
            flat(jnp.where(taken[i * half : (i + 1) * half],
                           placed[i * half : (i + 1) * half].astype(LOW),
                           base.reshape(half, rows, width)))
            for i, base in enumerate(grad_1)
        ]
        put_d = Scatter(links, [cross(active_1, grad_1)], w, order_a)
        grad_1, selected_grad, router_total = sync([put_d], grad_1, selected_grad, router_total)

        put_d.next()

        def back_ffn(i):
            grad = dot_back(grad_1[i], down_d)
            pre_grad = (gelu_parts(pre_1[i])[1] * grad).astype(LOW)
            return pre_grad, dot_back(pre_grad, up_d).astype(LOW)

        second = back_ffn(1)
        far = total_far(*halves(second[1]))
        first = back_ffn(0)
        near = total_core(*halves(first[1]))
        pre_grad_1 = [first[0], second[0]]
        put_u = Scatter(links, [cross(normed_1, pre_grad_1)], w, order_a)
        router_total = hop(router_total)
        near, far, router_total = sync([put_ra, put_u], near, far, router_total)

        put_u.next()
        put_ra.next()
        hits = (pos[:, None] == chosen[None, :]).astype(F32)
        middle_grad = result_grad.astype(F32) + jnp.dot(hits, selected_grad, precision=HIGH)
        hidden_grad = middle_grad + norm_back(
            hidden, scale_1, gains[1], near + far.astype(F32)
        )
        hidden_low = hidden_grad.astype(LOW)
        far = swap_far(hidden_low)
        grad_0 = [share_core(hidden_low)]
        first = attend_call(heads, grad_0[0], qkv_d, proj_d, bias_0[0], combined_0[0])
        router_total = hop(router_total)
        moving = [put_d]
        first, far, hidden_grad, router_total = sync(
            moving, first, far, hidden_grad, router_total
        )

        put_d.next()
        grad_0.append(share_core(far))
        second = attend_call(heads, grad_0[1], qkv_d, proj_d, bias_0[1], combined_0[1])
        proj_grad = proj_columns(cross(attended_0, grad_0))
        combined_grad_0 = [first[0], second[0]]
        put_a = Scatter(links, [cross(normed_0, combined_grad_0), proj_grad], w, order_a)
        router_total = hop(router_total)
        moving = [put_ra, put_d, put_u, put_a]
        first, second, router_total = sync(moving, first[1:], second[1:], router_total)

        put_a.next()
        put_u.next()
        put_d.next()
        put_ra.next()
        far_rf = swap_far(shard_r)
        far = total_far(*second)
        near = total_core(*first)
        input_part = norm_back(inputs, scale_0, gains[0], near + far.astype(F32))
        input_total = (hidden_grad + input_part).astype(LOW)
        added = jnp.dot(hits, rate[:, None] * change, precision=HIGH)
        result = (middle + added).astype(LOW)
        moving = [put_ra, put_d, put_u, put_a]
        input_total, result, router_total, far_rf = sync(
            moving, input_total, result, router_total, far_rf
        )

        def plans_f(weight):
            return [(0, wide, unit, weight), (unit_all, width, None, None)]

        def plans_a(weight):
            return [(0, 3, part, weight), (3 * part, 1, part, None)]

        put_a.next()
        put_u.next()
        shard_ra, shard_d = put_ra.finish(), put_d.finish()
        far_ra, far_d = swap_far(shard_ra), swap_far(shard_d)
        out_up_r, gain_ru, out_down_r = place(
            around(shard_r, far_rf), n, near_order, plans_f(routed_up)
        )
        while hops:
            router_total = hop(router_total)
        far_ra, far_d, gain_ru, router_total = sync(
            [put_a, put_u], far_ra, far_d, gain_ru, router_total
        )

        put_a.next()
        shard_u = put_u.finish()
        far_u = swap_far(shard_u)
        out_qkv_r, gain_ra, out_proj_r = place(
            around(shard_ra, far_ra), n, near_order, plans_a(routed_qkv)
        )
        (out_down,) = place(around(shard_d, far_d), n, near_order, [(0, width, None, None)])
        far_u, gain_ra, out_down = sync([put_a], far_u, gain_ra, out_down)

        shard_a = put_a.finish()
        far_a = swap_far(shard_a)
        out_up, gain_u = place(
            around(shard_u, far_u), n, near_order, [(0, wide, unit, dense_up)]
        )
        out_qkv, gain_a, out_proj = place(
            around(shard_a, far_a), n, near_order, plans_a(dense_qkv)
        )
        return (
            result[None],
            input_total[None],
            gain_grad(gain_a, dense_attn_gain),
            out_qkv,
            out_proj,
            gain_grad(gain_u, dense_mlp_gain),
            out_up,
            out_down,
            gain_grad(gain_ra, routed_attn_gain),
            out_qkv_r,
            out_proj_r,
            gain_grad(gain_ru, routed_mlp_gain),
            out_up_r,
            out_down_r,
            router_total,
        )

    return per_device


def solution(mesh):
    both = P(("wide", "narrow"))
    wide = P("wide")
    weights = (wide,) * 6
    return jax.shard_map(
        make_device(mesh.shape["wide"], mesh.shape["narrow"]),
        mesh=mesh,
        in_specs=(both, both, both, both) + weights + weights + (P(),),
        out_specs=(both, both) + weights + weights + (P(),),
        check_vma=False,
    )
```

```python
import functools

import jax
import jax.numpy as jnp
from jax import lax
from jax.experimental import pallas as pl
from jax.experimental.pallas import tpu as pltpu
from jax.sharding import PartitionSpec as P

HEADS = 16
EPS = 1e-06
NEG = -1e30
HIGH = lax.Precision.HIGHEST
LOW = jnp.bfloat16
F32 = jnp.float32
I32 = jnp.int32
VMEM_SPEC = pl.BlockSpec(memory_space=pltpu.VMEM)
SMEM_SPEC = pl.BlockSpec(memory_space=pltpu.SMEM)
ANY_SPEC = pl.BlockSpec(memory_space=pl.ANY)


def dot_rows(left, right):
    return jnp.dot(left, right, preferred_element_type=F32)


def dot_cross(left, right):
    return lax.dot_general(left, right, (((0,), (0,)), ((), ())), preferred_element_type=F32)


def dot_back(left, right):
    return lax.dot_general(left, right, (((1,), (1,)), ((), ())), preferred_element_type=F32)


def bits_of(size):
    found = []
    bit = size // 2
    while bit >= 1:
        found.append(bit)
        bit //= 2
    return found


def xor_blocks(array, index, blocks, axis):
    size = array.shape[axis] // blocks
    for bit in bits_of(blocks):
        parts = [
            lax.slice_in_dim(array, k * size, (k + 1) * size, axis=axis) for k in range(blocks)
        ]
        swapped = jnp.concatenate([parts[k ^ bit] for k in range(blocks)], axis=axis)
        array = jnp.where((index & bit) != 0, swapped, array)
    return array


class Links:
    def __init__(self, sizes):
        self.sizes = sizes

    def swap(self, array, axis, bit):
        return lax.ppermute(array, axis, [(i, i ^ bit) for i in range(self.sizes[axis])])

    def gather(self, local, axis, order):
        for bit in order:
            local = jnp.concatenate([local, self.swap(local, axis, bit)], 0)
        return local


class Gather:
    def __init__(self, links, piece, order):
        self.links = links
        self.arrays = [piece]
        self.offsets = [[0]]
        self.todo = [(order[0], None)]
        made = 1
        for bit in order[1:]:
            self.todo += [(bit, i) for i in range(made)]
            made *= 2

    def next(self, count=1):
        for bit, at in self.todo[:count]:
            got = self.links.swap(self.arrays[at or 0], "wide", bit)
            offsets = [k ^ bit for k in self.offsets[at or 0]]
            if at is None:
                self.arrays = [jnp.concatenate([self.arrays[0], got], 0)]
                self.offsets = [self.offsets[0] + offsets]
            else:
                self.arrays.append(got)
                self.offsets.append(offsets)
        self.todo = self.todo[count:]

    def finish(self):
        self.next(len(self.todo))
        return list(zip(self.offsets, self.arrays))


class Scatter:
    def __init__(self, links, columns, index, order):
        self.links = links
        self.index = index
        self.bits = bits_of(links.sizes["wide"])
        self.left = list(order[::-1])
        lead = (2,) * len(self.bits)
        size = links.sizes["wide"]
        self.base = [c.reshape(lead + (c.shape[0] // size, c.shape[1])) for c in columns]
        self.got = None
        self.at = None
        self.mine = None

    @property
    def arrays(self):
        return [self.base] if self.got is None else [self.base, self.got]

    @arrays.setter
    def arrays(self, values):
        self.base = values[0]
        if self.got is not None:
            self.got = values[1]

    def value(self):
        def pick(c):
            return lax.dynamic_index_in_dim(c, self.mine, self.at, keepdims=False)

        if self.got is None:
            return jnp.concatenate(self.base, -1) if len(self.base) > 1 else self.base[0]
        kept = jnp.concatenate([pick(c) for c in self.base], -1)
        return (kept.astype(F32) + self.got.astype(F32)).astype(LOW)

    def next(self):
        if not self.left:
            return
        bit = self.left.pop(0)
        at = self.bits.index(bit)
        mine = jnp.where((self.index & bit) != 0, 1, 0).astype(I32)
        if self.got is not None:
            self.base = [self.value()]
        send = jnp.concatenate(
            [lax.dynamic_index_in_dim(c, 1 - mine, at, keepdims=False) for c in self.base], -1
        )
        self.bits.pop(at)
        self.at, self.mine = at, mine
        self.got = self.links.swap(send, "wide", bit)

    def finish(self):
        while self.left:
            self.next()
        return self.value()


def sync(movers, *values):
    held = lax.optimization_barrier(([m.arrays for m in movers], values))
    for mover, arrays in zip(movers, held[0]):
        mover.arrays = arrays
    return held[1]


def order_of(order):
    offsets = [0]
    for bit in order:
        offsets = offsets + [k ^ bit for k in offsets]
    return offsets


def pack(index, narrow, shards, layouts):
    def kernel(index_ref, *refs):
        ins, outs, sems = refs[: len(shards)], refs[len(shards) : -1], refs[-1]
        at = index_ref[0]
        copies = []

        def add(source, target):
            copies.append(pltpu.make_async_copy(source, target, sems.at[len(copies)]))

        for (out, members), out_ref in zip(layouts, outs):
            low = 0
            for member, blocks, width in members:
                source = ins[member]
                if blocks is None:
                    size = source.shape[0] // narrow
                    row = pl.multiple_of(at * size, size)
                    cols = source.shape[1]
                    add(source.at[pl.ds(row, size), :], out_ref.at[0, :, low : low + cols])
                    low += cols
                    continue
                for block in range(blocks):
                    start = pl.multiple_of((block * narrow + at) * width, width)
                    add(source.at[:, pl.ds(start, width)], out_ref.at[0, :, low : low + width])
                    low += width
        for copy in copies:
            copy.start()
        for copy in copies:
            copy.wait()

    count = sum(1 if m[1] is None else m[1] for _, members in layouts for m in members)
    return pl.pallas_call(
        kernel,
        out_shape=[jax.ShapeDtypeStruct((1,) + shape, LOW) for shape, _ in layouts],
        in_specs=[SMEM_SPEC] + [ANY_SPEC] * len(shards),
        out_specs=[VMEM_SPEC] * len(layouts),
        scratch_shapes=[pltpu.SemaphoreType.DMA((count,))],
    )(index.reshape(1), *shards)


def assemble(sources, index, widths):
    own = sources[0][0][0][1].shape[1]
    arrays = [array for parts, _ in sources for _, array in parts]
    rows = sum(len(ks) for ks, _ in sources[0][0]) * own
    count = sum(len(ks) * len(spans) for parts, spans in sources for ks, _ in parts)

    def kernel(index_ref, *refs):
        ins, outs, sems = refs[: len(arrays)], refs[len(arrays) : -1], refs[-1]
        copies = []
        at_ref = 0
        for parts, spans in sources:
            for ks, _ in parts:
                for j, k in enumerate(ks):
                    row = pl.multiple_of((index_ref[0] ^ k) * own, own)
                    for low, high, out, at in spans:
                        copies.append(
                            pltpu.make_async_copy(
                                ins[at_ref].at[j, :, low:high],
                                outs[out].at[pl.ds(row, own), at : at + high - low],
                                sems.at[len(copies)],
                            )
                        )
                at_ref += 1
        for copy in copies:
            copy.start()
        for copy in copies:
            copy.wait()

    return pl.pallas_call(
        kernel,
        out_shape=[jax.ShapeDtypeStruct((rows, width), LOW) for width in widths],
        in_specs=[SMEM_SPEC] + [ANY_SPEC] * len(arrays),
        out_specs=[VMEM_SPEC] * len(widths),
        scratch_shapes=[pltpu.SemaphoreType.DMA((count,))],
    )(index.reshape(1), *arrays)


def head_columns(ref, part, head, heads, width):
    start = (part * heads + head) * width
    return ref[:, start : start + width]


def head_prob(query, key, bias):
    scores = dot_back(query, key) + bias
    lifted = jnp.exp(scores - jnp.max(scores, -1, keepdims=True))
    return lifted / jnp.sum(lifted, -1, keepdims=True)


def write_part(part_refs, value):
    for i, ref in enumerate(part_refs):

        @pl.when(pl.program_id(0) == i)
        def _():
            ref[...] = value


def attend_kernel(
    heads, normed_ref, qkv_ref, proj_ref, bias_ref, combined_ref, out_ref, *part_refs
):
    width = out_ref.shape[1] // heads
    bias = bias_ref[0]
    combined_ref[...] = dot_rows(normed_ref[...], qkv_ref[...]).astype(LOW)
    outs = []
    for head in range(heads):
        query = head_columns(combined_ref, 0, head, heads, width) * LOW(width**-0.5)
        key = head_columns(combined_ref, 1, head, heads, width)
        val = head_columns(combined_ref, 2, head, heads, width)
        prob = head_prob(query, key, bias).astype(LOW)
        outs.append(dot_rows(prob, val).astype(LOW))
    attended = jnp.concatenate(outs, 1)
    out_ref[...] = attended
    write_part(part_refs, dot_rows(attended, proj_ref[...]).astype(LOW))


def attend_back_kernel(
    heads, grad_ref, qkv_ref, proj_ref, bias_ref, combined_ref, out_ref, *rest
):
    part_refs, low_ref = rest[:-1], rest[-1]
    width = low_ref.shape[1] // heads
    scale = width**-0.5
    bias = bias_ref[0]
    low_ref[...] = dot_back(grad_ref[...], proj_ref[...]).astype(LOW)
    outs = [[], [], []]
    for head in range(heads):
        query = head_columns(combined_ref, 0, head, heads, width) * LOW(scale)
        key = head_columns(combined_ref, 1, head, heads, width)
        val = head_columns(combined_ref, 2, head, heads, width)
        grad = head_columns(low_ref, 0, head, heads, width)
        prob = head_prob(query, key, bias)
        prob_grad = dot_back(grad, val)
        inner = jnp.sum(prob * prob_grad, -1, keepdims=True)
        score_grad = (prob * (prob_grad - inner)).astype(LOW)
        outs[0].append((dot_rows(score_grad, key) * scale).astype(LOW))
        outs[1].append(dot_cross(score_grad, query).astype(LOW))
        outs[2].append(dot_cross(prob.astype(LOW), grad).astype(LOW))
    combined_grad = jnp.concatenate(outs[0] + outs[1] + outs[2], 1)
    out_ref[...] = combined_grad
    write_part(part_refs, dot_back(combined_grad, qkv_ref[...]).astype(LOW))


def attend_call(heads, values, qkv, proj, bias, combined=None):
    groups, rows, _ = bias.shape
    width = values.shape[1]
    third = proj.shape[0]
    total = groups * rows

    def rows_spec(cols):
        return pl.BlockSpec((rows, cols), lambda i: (i, 0))

    def whole_spec(array):
        return pl.BlockSpec(array.shape, lambda i: (0, 0))

    bias_spec = pl.BlockSpec((1, rows, rows), lambda i: (i, 0, 0))
    in_specs = [rows_spec(width), whole_spec(qkv), whole_spec(proj), bias_spec]
    wide_out = jax.ShapeDtypeStruct((total, 3 * third), LOW)
    part_outs = [jax.ShapeDtypeStruct((rows, width), LOW)] * groups
    part_specs = [pl.BlockSpec((rows, width), lambda i: (0, 0))] * groups
    if combined is None:
        return pl.pallas_call(
            functools.partial(attend_kernel, heads),
            grid=(groups,),
            out_shape=[wide_out, jax.ShapeDtypeStruct((total, third), LOW)] + part_outs,
            in_specs=in_specs,
            out_specs=[rows_spec(3 * third), rows_spec(third)] + part_specs,
        )(values, qkv, proj, bias)
    return pl.pallas_call(
        functools.partial(attend_back_kernel, heads),
        grid=(groups,),
        out_shape=[wide_out] + part_outs,
        in_specs=in_specs + [rows_spec(3 * third)],
        out_specs=[rows_spec(3 * third)] + part_specs,
        scratch_shapes=[pltpu.VMEM((rows, third), LOW)],
    )(values, qkv, proj, bias, combined)


def tile_call(body, outs, tiled, whole):
    rows = tiled[0].shape[0]
    block = min(rows, 128)
    count = len(tiled) + len(whole)

    def kernel(*refs):
        results = body(*[ref[...] for ref in refs[:count]])
        for ref, result in zip(refs[count:], results):
            ref[...] = result

    def rows_spec(cols):
        return pl.BlockSpec((block, cols), lambda i: (i, 0))

    return pl.pallas_call(
        kernel,
        grid=(rows // block,),
        out_shape=[jax.ShapeDtypeStruct((rows, cols), dtype) for cols, dtype in outs],
        in_specs=[rows_spec(t.shape[1]) for t in tiled]
        + [pl.BlockSpec(t.shape, lambda i: (0, 0)) for t in whole],
        out_specs=[rows_spec(cols) for cols, _ in outs],
    )(*tiled, *whole)


def cross(lefts, rights):
    out = dot_cross(lefts[0], rights[0])
    for left, right in zip(lefts[1:], rights[1:]):
        out = out + dot_cross(left, right)
    return out.astype(LOW)


def place(entries, index, order, plans):
    count = len(entries)
    own = entries[0].shape[0]
    weights = [plan[3] for plan in plans if plan[3] is not None]

    def kernel(index_ref, *refs):
        parts, weight_refs = refs[:count], list(refs[count : count + len(weights)])
        outs = list(refs[count + len(weights) :])

        def write(j, part_ref, out_refs):
            for (first, pieces, chunk, _), out_ref in zip(plans, out_refs):
                if chunk is None:
                    rows = pl.ds(pl.multiple_of(j * own, own), own)
                    out_ref[rows, :] = part_ref[:, first : first + pieces].astype(F32)
                    continue
                for p in range(pieces if chunk % 128 == 0 else 0):
                    at = pl.ds(pl.multiple_of((p * count + j) * chunk, chunk), chunk)
                    low = first + p * chunk
                    out_ref[:, at] = part_ref[:, low : low + chunk].astype(F32)

        def narrow_chunks(index, parts, out_ref, first, pieces, chunk):
            for j in range(count):
                for p in range(pieces):
                    low = first + p * chunk
                    value = parts[0][:, low : low + chunk].astype(F32)
                    for k, part_ref in zip(order[1:], parts[1:]):
                        other = part_ref[:, low : low + chunk].astype(F32)
                        value = jnp.where((index ^ j) == k, other, value)
                    at = (p * count + j) * chunk
                    out_ref[:, at : at + chunk] = value

        out_refs, sum_refs = [], []
        for plan in plans:
            out_refs.append(outs.pop(0))
            sum_refs.append(outs.pop(0) if plan[3] is not None else None)
        for k, part_ref in zip(order, parts):
            write(index_ref[0] ^ k, part_ref, out_refs)
        for (first, pieces, chunk, _), out_ref in zip(plans, out_refs):
            if chunk is not None and chunk % 128:
                narrow_chunks(index_ref[0], parts, out_ref, first, pieces, chunk)
        for out_ref, sum_ref in zip(out_refs, sum_refs):
            if sum_ref is not None:
                weight = weight_refs.pop(0)[...].astype(F32)
                sum_ref[...] = jnp.sum(weight * out_ref[...], -1, keepdims=True)

    shapes = []
    for _, pieces, chunk, weight in plans:
        if chunk is None:
            shapes.append((count * own, pieces))
        else:
            shapes.append((own, pieces * count * chunk))
        if weight is not None:
            shapes.append((own, 1))
    return pl.pallas_call(
        kernel,
        out_shape=[jax.ShapeDtypeStruct(shape, F32) for shape in shapes],
        in_specs=[SMEM_SPEC] + [VMEM_SPEC] * (count + len(weights)),
        out_specs=[VMEM_SPEC] * len(shapes),
    )(index.reshape(1), *entries, *weights)


def norm_stats(values):
    return lax.rsqrt(jnp.mean(values * values, -1, keepdims=True) + EPS)


def norm_back(values, scale, gain, grad):
    weighted = grad * gain
    inner = jnp.mean(weighted * values, -1, keepdims=True)
    return scale * (weighted - values * (scale * scale) * inner)


def gelu_parts(v):
    root = 0.7978845608028654
    inner = jnp.tanh(root * (v + 0.044715 * v * v * v))
    value = 0.5 * v * (1.0 + inner)
    slope = 0.5 * (1.0 + inner) + 0.5 * v * (1.0 - inner * inner) * root * (
        1.0 + 3.0 * 0.044715 * v * v
    )
    return value, slope


def make_device(wide, narrow):
    wide_bits = bits_of(wide)
    narrow_bits = bits_of(narrow)
    order_a = list(wide_bits)
    order_c = wide_bits[-1:] + wide_bits[:-1]
    near_order = order_of(narrow_bits)

    def per_device(
        tokens,
        segment_ids,
        routed_index,
        out_grad,
        dense_attn_gain,
        dense_qkv,
        dense_proj,
        dense_mlp_gain,
        dense_up,
        dense_down,
        routed_attn_gain,
        routed_qkv,
        routed_proj,
        routed_mlp_gain,
        routed_up,
        routed_down,
        router_vector,
    ):
        links = Links({"wide": wide, "narrow": narrow})
        w = lax.axis_index("wide").astype(I32)
        n = lax.axis_index("narrow").astype(I32)
        inputs = tokens[0].astype(F32)
        rows, width = inputs.shape
        segments = segment_ids[0]
        chosen = routed_index[0]
        cap = chosen.shape[0]
        heads = HEADS // narrow
        own = width // wide
        ffn = dense_up.shape[1]
        part = width // narrow
        unit = ffn // (wide * narrow)

        def pack_some(shards, kinds):
            def up_of(member):
                shard = shards[member].reshape(own, wide, narrow, unit)
                piece = lax.dynamic_index_in_dim(shard, n, 2, keepdims=False)
                return piece.reshape(own, ffn // narrow)

            def down_of(member):
                shard = shards[member].reshape(narrow, unit, width)
                return lax.dynamic_index_in_dim(shard, n, 0, keepdims=False)

            def attn_of(member):
                mixed = jnp.concatenate([shards[member], shards[member + 1]], 1)
                mixed = mixed.reshape(own, 4, narrow, part)
                piece = lax.dynamic_index_in_dim(mixed, n, 2, keepdims=False)
                return piece.reshape(own, 4 * part)

            layouts, pieces, member = [], [], 0
            for kind in kinds:
                if kind == "a":
                    members = [(member, 3, part), (member + 1, 1, part)]
                    layouts.append(((own, 4 * part), members))
                    pieces.append(lambda m=member: attn_of(m))
                elif kind == "u":
                    layouts.append(((own, ffn // narrow), [(member, wide, unit)]))
                    pieces.append(lambda m=member: up_of(m))
                else:
                    layouts.append(((unit, width), [(member, None, None)]))
                    pieces.append(lambda m=member: down_of(m))
                member += 2 if kind == "a" else 1
            if unit % 128 == 0:
                return pack(n, narrow, shards, layouts)
            return [piece()[None] for piece in pieces]

        def swap_blocks(array, axis):
            got = []
            for k in range(narrow):
                block = lax.dynamic_slice_in_dim(array, (n ^ k) * part, part, axis)
                got.append(block if k == 0 else links.swap(block, "narrow", k))
            return got

        def open_proj(proj_cols):
            return xor_blocks(jnp.concatenate(swap_blocks(proj_cols, 0), 1), n, narrow, 1)

        def open_rows(parts, columns):
            return assemble([(parts, [(0, columns, 0, 0)])], w, (columns,))[0]

        def proj_columns(proj_grad):
            return xor_blocks(jnp.concatenate(swap_blocks(proj_grad, 1), 0), n, narrow, 0)

        def flat(array):
            return array.reshape(-1, array.shape[-1])

        def share_core(local):
            return jnp.concatenate([local, links.swap(local, "narrow", 1)], 0)

        def swap_far(local):
            return links.swap(local, "narrow", 2)

        def share(local):
            got = [local] + [links.swap(local, "narrow", k) for k in range(1, narrow)]
            return jnp.stack(got, 0)

        def total(whole):
            parts = whole.reshape(narrow, -1, width)
            out = parts[0].astype(F32)
            for k in range(1, narrow):
                out = out + links.swap(parts[k], "narrow", k).astype(F32)
            return out

        def total_core(keep, send):
            return keep.astype(F32) + links.swap(send, "narrow", 1).astype(F32)

        def total_far(keep, send):
            return swap_far(total_core(keep, send).astype(LOW))

        def halves(chunk):
            half = chunk.shape[0] // 2
            return chunk[:half], chunk[half:]

        def normed_of(values, scale, gain):
            return (values * scale * gain).astype(LOW)

        def up_body(normed, up):
            pre = dot_rows(normed, up)
            return pre, gelu_parts(pre)[0].astype(LOW)

        def both_body(normed, grad, up, down):
            pre = dot_rows(normed, up)
            value, slope = gelu_parts(pre)
            active = value.astype(LOW)
            pre_grad = (slope * dot_back(grad, down)).astype(LOW)
            part = dot_back(pre_grad, up).astype(LOW)
            return active, dot_rows(active, down).astype(LOW), pre_grad, part

        def gain_grad(sums, gain):
            return sums[:, 0] / gain.astype(F32)

        def around(shard, far):
            others = [links.swap(part, "narrow", 1) for part in (shard, far)]
            return [shard, far] + others

        unit_all = ffn // narrow

        (piece_a,) = pack_some([dense_qkv, dense_proj], "a")
        split = 2 * part
        get_a = Gather(links, piece_a[:, :, :split], order_a)
        get_b = Gather(links, piece_a[:, :, split:], order_c)
        get_a.next()
        get_b.next()
        gains = jnp.stack([dense_attn_gain, dense_mlp_gain, routed_attn_gain, routed_mlp_gain])
        gains = links.gather(gains[None], "wide", order_a[:1])
        (gains,) = sync([get_a, get_b], gains)

        get_a.next(2)
        get_b.next()
        gains = links.gather(gains, "wide", order_a[1:])
        marks = share(jnp.concatenate([segments, chosen, jnp.take(segments, chosen)]))
        scale_0 = norm_stats(inputs)
        piece_u, piece_d, *pieces_r = pack_some(
            [dense_up, dense_down, routed_qkv, routed_proj, routed_up, routed_down], "udaud"
        )
        get_u = Gather(links, piece_u, order_a)
        get_d = Gather(links, piece_d, order_a)
        everything = [get_a, get_b, get_u, get_d]
        gains, scale_0, marks = sync(everything, gains, scale_0, marks)

        get_a.next()
        get_b.next(2)
        get_u.next()
        spread = order_of(order_a)
        places = jnp.array([spread.index(k) for k in range(wide)], I32)
        gains = jnp.take(gains, places[w ^ jnp.arange(wide, dtype=I32)], axis=0)
        gains = gains.transpose(1, 0, 2).reshape(4, width).astype(F32)
        normed = normed_of(inputs, scale_0, gains[0])
        far = swap_far(normed)
        normed_0 = [share_core(normed)]
        seg_all = marks[:, :rows]
        pos_r = marks[:, rows : rows + cap]
        seg_r = marks[:, rows + cap :].reshape(-1)
        where_r, of_r = pos_r.reshape(-1), jnp.repeat(jnp.arange(narrow, dtype=I32), cap)
        pos = jnp.arange(rows, dtype=I32)
        allowed = (pos[None, None, :] <= pos[None, :, None]) & (
            seg_all[:, None, :] == seg_all[:, :, None]
        )
        bias_0 = jnp.where(allowed, 0.0, NEG).astype(F32)
        bias_0 = [bias_0[: narrow // 2], bias_0[narrow // 2 :]]
        allowed = (where_r[None, :] <= where_r[:, None]) & (seg_r[None, :] == seg_r[:, None])
        allowed = allowed & (of_r[None, :] == of_r[:, None])
        bias_r = jnp.where(allowed, 0.0, NEG).astype(F32)[None]
        hits_all = (pos[None, :, None] == pos_r[:, None, :]).astype(LOW)
        gains, far, normed_0, bias_0, bias_r, hits_all, pieces_r = sync(
            everything, gains, far, normed_0, bias_0, bias_r, hits_all, pieces_r
        )
        full_ra, up_r, down_r = [
            lax.all_gather(piece[0], "wide", axis=0, tiled=True) for piece in pieces_r
        ]

        get_u.next(2)
        get_d.next()
        normed_0.append(share_core(far))
        qkv_d, proj_d = assemble(
            [
                (get_a.finish(), [(0, split, 0, 0)]),
                (get_b.finish(), [(0, part, 0, split), (part, 2 * part, 1, 0)]),
            ],
            w,
            (3 * part, part),
        )
        proj_d = open_proj(proj_d)
        second = attend_call(heads, normed_0[1], qkv_d, proj_d, bias_0[1])
        everything = [get_u, get_d]
        second, qkv_d, proj_d = sync(everything, second, qkv_d, proj_d)

        get_u.next()
        get_d.next()
        far = total_far(*second[2:])
        first = attend_call(heads, normed_0[0], qkv_d, proj_d, bias_0[0])
        combined_0 = [first[0], second[0]]
        attended_0 = [first[1], second[1]]
        near = total_core(*first[2:])
        near, far = sync(everything, near, far)

        get_d.next()
        hidden = inputs + near + far.astype(F32)
        scale_1 = norm_stats(hidden)
        normed = normed_of(hidden, scale_1, gains[1])
        far = swap_far(normed)
        normed_1 = [share_core(normed)]
        up_d = open_rows(get_u.finish(), unit_all)
        everything = everything[1:]
        first = tile_call(up_body, [(unit_all, F32), (unit_all, LOW)], normed_1, [up_d])
        first, far, up_d, hidden, scale_1 = sync(everything, first, far, up_d, hidden, scale_1)

        get_d.next()
        normed_1.append(share_core(far))
        second = tile_call(up_body, [(unit_all, F32), (unit_all, LOW)], [normed_1[1]], [up_d])
        pre_1 = [first[0], second[0]]
        active_1 = [first[1], second[1]]
        active_1, pre_1 = sync(everything, active_1, pre_1)

        down_d = open_rows(get_d.finish(), width)
        far = total_far(*[dot_rows(a, down_d).astype(LOW) for a in halves(active_1[1])])
        near = total_core(*[dot_rows(a, down_d).astype(LOW) for a in halves(active_1[0])])
        near, far, down_d = sync([], near, far, down_d)

        middle = hidden + near + far.astype(F32)
        selected = jnp.take(middle, chosen, axis=0)
        route_vec = router_vector.astype(F32)
        rate = jax.nn.sigmoid(jnp.dot(selected, route_vec, precision=HIGH))
        result_grad = out_grad[0]
        picked_grad = jnp.take(result_grad, chosen, axis=0).astype(F32)
        change_grad = rate[:, None] * picked_grad
        scale_2 = norm_stats(selected)
        normed_2 = flat(share(normed_of(selected, scale_2, gains[2])))
        qkv_r, proj_r = full_ra[:, : 3 * part], open_proj(full_ra[:, 3 * part :])
        combined_2, attended_2, part_2 = attend_call(heads, normed_2, qkv_r, proj_r, bias_r)
        routed_att = total(part_2)
        grad_3 = flat(share(change_grad.astype(LOW)))
        after = selected + routed_att
        scale_3 = norm_stats(after)
        normed_3 = flat(share(normed_of(after, scale_3, gains[3])))
        grad_1 = [share_core(result_grad), share_core(swap_far(result_grad))]

        active_3, routed_out, pre_grad_3, normed_part = tile_call(
            both_body,
            [(unit_all, LOW), (width, LOW), (unit_all, LOW), (width, LOW)],
            [normed_3, grad_3],
            [up_r, down_r],
        )
        both_r = jnp.concatenate(
            [cross([normed_3], [pre_grad_3]), cross([active_3], [grad_3])], 1
        )
        both_r, normed_part, routed_out, grad_1 = sync(
            [], both_r, normed_part, routed_out, grad_1
        )
        shard_r = lax.psum_scatter(both_r, "wide", scatter_dimension=0, tiled=True)

        after_grad = norm_back(after, scale_3, gains[3], total(normed_part))
        grad_2 = flat(share((change_grad + after_grad).astype(LOW)))
        proj_grad = proj_columns(cross([attended_2], [grad_2]))
        combined_grad_2, part_2 = attend_call(heads, grad_2, qkv_r, proj_r, bias_r, combined_2)
        change = routed_att + total(routed_out)
        put_ra = Scatter(links, [cross([normed_2], [combined_grad_2]), proj_grad], w, order_c)
        part_2, change = sync([put_ra], part_2, change)

        put_ra.next()
        rate_grad = jnp.sum(picked_grad * change, -1)
        logit_grad = rate_grad * rate * (1.0 - rate)
        att_in_grad = norm_back(selected, scale_2, gains[2], total(part_2))
        selected_grad = after_grad + att_in_grad + logit_grad[:, None] * route_vec[None, :]
        fresh = share((picked_grad + selected_grad).astype(LOW))
        router_total = jnp.dot(logit_grad, selected, precision=HIGH)
        hops = [("wide", bit) for bit in wide_bits[:-1]]
        hops += [("narrow", bit) for bit in narrow_bits[::-1]] + [("wide", wide_bits[-1])]

        def hop(value):
            if hops:
                value = value + links.swap(value, *hops.pop(0))
            return value

        router_total = hop(router_total)
        placed = jnp.einsum("sqk,skd->sqd", hits_all, fresh, preferred_element_type=F32)
        taken = jnp.any(hits_all != 0, -1, keepdims=True)
        half = narrow // 2
        grad_1 = [
            flat(jnp.where(taken[i * half : (i + 1) * half],
                           placed[i * half : (i + 1) * half].astype(LOW),
                           base.reshape(half, rows, width)))
            for i, base in enumerate(grad_1)
        ]
        put_d = Scatter(links, [cross(active_1, grad_1)], w, order_a)
        grad_1, selected_grad, router_total = sync([put_d], grad_1, selected_grad, router_total)

        put_d.next()

        def back_ffn(i):
            grad = dot_back(grad_1[i], down_d)
            pre_grad = (gelu_parts(pre_1[i])[1] * grad).astype(LOW)
            return pre_grad, dot_back(pre_grad, up_d).astype(LOW)

        second = back_ffn(1)
        far = total_far(*halves(second[1]))
        first = back_ffn(0)
        near = total_core(*halves(first[1]))
        pre_grad_1 = [first[0], second[0]]
        put_u = Scatter(links, [cross(normed_1, pre_grad_1)], w, order_a)
        router_total = hop(router_total)
        near, far, router_total = sync([put_ra, put_u], near, far, router_total)

        put_u.next()
        put_ra.next()
        hits = (pos[:, None] == chosen[None, :]).astype(F32)
        middle_grad = result_grad.astype(F32) + jnp.dot(hits, selected_grad, precision=HIGH)
        hidden_grad = middle_grad + norm_back(
            hidden, scale_1, gains[1], near + far.astype(F32)
        )
        hidden_low = hidden_grad.astype(LOW)
        far = swap_far(hidden_low)
        grad_0 = [share_core(hidden_low)]
        first = attend_call(heads, grad_0[0], qkv_d, proj_d, bias_0[0], combined_0[0])
        router_total = hop(router_total)
        moving = [put_d]
        first, far, hidden_grad, router_total = sync(
            moving, first, far, hidden_grad, router_total
        )

        put_d.next()
        grad_0.append(share_core(far))
        second = attend_call(heads, grad_0[1], qkv_d, proj_d, bias_0[1], combined_0[1])
        proj_grad = proj_columns(cross(attended_0, grad_0))
        combined_grad_0 = [first[0], second[0]]
        put_a = Scatter(links, [cross(normed_0, combined_grad_0), proj_grad], w, order_a)
        router_total = hop(router_total)
        moving = [put_ra, put_d, put_u, put_a]
        first, second, router_total = sync(moving, first[1:], second[1:], router_total)

        put_a.next()
        put_u.next()
        put_d.next()
        far_rf = swap_far(shard_r)
        far = total_far(*second)
        near = total_core(*first)
        input_part = norm_back(inputs, scale_0, gains[0], near + far.astype(F32))
        input_total = (hidden_grad + input_part).astype(LOW)
        added = jnp.dot(hits, rate[:, None] * change, precision=HIGH)
        result = (middle + added).astype(LOW)
        moving = [put_ra, put_d, put_u, put_a]
        input_total, result, router_total, far_rf = sync(
            moving, input_total, result, router_total, far_rf
        )

        def plans_f(weight):
            return [(0, wide, unit, weight), (unit_all, width, None, None)]

        def plans_a(weight):
            return [(0, 3, part, weight), (3 * part, 1, part, None)]

        put_a.next()
        put_u.next()
        put_ra.next()
        shard_d = put_d.finish()
        far_d = swap_far(shard_d)
        out_up_r, gain_ru, out_down_r = place(
            around(shard_r, far_rf), n, near_order, plans_f(routed_up)
        )
        while hops:
            router_total = hop(router_total)
        far_d, gain_ru, router_total = sync(
            [put_a, put_u, put_ra], far_d, gain_ru, router_total
        )

        put_a.next()
        shard_u, shard_ra = put_u.finish(), put_ra.finish()
        far_u, far_ra = swap_far(shard_u), swap_far(shard_ra)
        (out_down,) = place(around(shard_d, far_d), n, near_order, [(0, width, None, None)])
        far_u, far_ra, out_down = sync([put_a], far_u, far_ra, out_down)

        shard_a = put_a.finish()
        far_a = swap_far(shard_a)
        out_qkv_r, gain_ra, out_proj_r = place(
            around(shard_ra, far_ra), n, near_order, plans_a(routed_qkv)
        )
        out_up, gain_u = place(
            around(shard_u, far_u), n, near_order, [(0, wide, unit, dense_up)]
        )
        out_qkv, gain_a, out_proj = place(
            around(shard_a, far_a), n, near_order, plans_a(dense_qkv)
        )
        return (
            result[None],
            input_total[None],
            gain_grad(gain_a, dense_attn_gain),
            out_qkv,
            out_proj,
            gain_grad(gain_u, dense_mlp_gain),
            out_up,
            out_down,
            gain_grad(gain_ra, routed_attn_gain),
            out_qkv_r,
            out_proj_r,
            gain_grad(gain_ru, routed_mlp_gain),
            out_up_r,
            out_down_r,
            router_total,
        )

    return per_device


def solution(mesh):
    both = P(("wide", "narrow"))
    wide = P("wide")
    weights = (wide,) * 6
    return jax.shard_map(
        make_device(mesh.shape["wide"], mesh.shape["narrow"]),
        mesh=mesh,
        in_specs=(both, both, both, both) + weights + weights + (P(),),
        out_specs=(both, both) + weights + weights + (P(),),
        check_vma=False,
    )
```
